128 devices in a mesh: band: 8 (over y, z_hi), plane: 16 (over z_lo, x, core).
Axes of the slice: x: 4, y: 4, z: 4 (z_hi: 2, z_lo: 2; z = z_hi * 2 + z_lo), core: 2. Of those that a mesh axis runs over, the one named last changes fastest.
Arguments:
- orbitals: float32 [64, 96, 9216], P('band', 'plane'), may hold values from -6 to 6
Outputs:
- exchange_action: float32 [64, 96, 9216], P('band', 'plane')
The draws below stay inside these ranges and needn't reach their ends.
All inputs are finite; a program needn't handle non-finite values.
Results may differ from the reference program's by a relative error of at most 0.0001.
Values sent between devices are 32-bit elements; how exact they have to be, the bound alone decides.
A program may use at most 128 MiB of HBM per device.

```python
import math
import jax
import jax.numpy as jnp
from jax import lax

NG = 96
LB = 8
PAIR = 2
ROUNDS = 4
NBANDS = 64


def block_scale(own_key, shape, cuts, low, largest):
    loudness, own = 1.0, jax.random.fold_in(own_key, 6)
    for dim, shards_of in cuts:
        heights = jnp.exp(jax.random.uniform(jax.random.fold_in(own, dim), (shards_of,), jnp.float32, low / len(cuts), largest / len(cuts)))
        loudness = loudness * jnp.repeat(heights, shape[dim] // shards_of).reshape([-1 if axis == dim else 1 for axis in range(len(shape))])
    return loudness


def noise(rng, dims, spread, limit, shards=(), held_as=jnp.bfloat16):
    factor_of = block_scale(rng, dims, shards, -0.22, 0.18) if shards else 1.0
    array = jax.random.normal(rng, dims, jnp.float32) * spread * factor_of
    return jnp.minimum(jnp.maximum(array, -limit), limit).astype(held_as)


def setup_inputs(seed: int = 0) -> dict:
    keys = jax.random.split(jax.random.key(seed), 2)
    return {
        "orbitals": noise(keys[0], (NBANDS, NG, NG * NG), 1.0, 6.0, ((0, 8), (1, 16)), jnp.float32),
    }


OMEGA = 0.106
CELL = 41.05
ALPHA = 0.25


def frequencies(count):
    index = jnp.arange(count)
    return jnp.where(index <= count // 2, index, index - count).astype(jnp.float32)


def screened(count):
    freq = frequencies(count)
    square = freq * freq
    scale = (2.0 * math.pi / CELL) ** 2
    g_two = scale * (square[:, None, None] + square[None, :, None] + square[None, None, :])
    positive = g_two > 0
    safe = jnp.where(positive, g_two, 1.0)
    value = 4.0 * math.pi / safe * (-jnp.expm1(-safe / (4.0 * OMEGA * OMEGA)))
    return jnp.where(positive, value, math.pi / (OMEGA * OMEGA))


def reference(orbitals):
    nbands = orbitals.shape[0]
    fields = orbitals.reshape(nbands, NG, NG, NG)
    kernel = screened(NG)

    def solve(density):
        return jnp.real(jnp.fft.ifftn(kernel * jnp.fft.fftn(density)))

    total = jnp.zeros_like(fields)
    for turn in range(ROUNDS):
        for member in range(PAIR):
            partner_index = turn * LB + member
            partner = fields[partner_index]

            def single_pair(single):
                potential = solve(single * partner).astype(fields.dtype)
                return partner * potential, single * potential

            near_terms, far_terms = lax.map(single_pair, fields)
            total = total + near_terms
            total = total.at[partner_index].add(jnp.sum(far_terms, axis=0))
    return (-ALPHA * total).reshape(nbands, NG, NG * NG)
```

```python
import math, functools
import numpy as np
import jax, jax.numpy as jnp
from jax import lax
from jax.experimental import pallas as pl
from jax.experimental.pallas import tpu as pltpu
from jax.sharding import PartitionSpec as P
import ml_dtypes

N = 96
OMEGA = 0.106
CELL = 41.05
bf = jnp.bfloat16

def split_np(t):
    t = t.astype(np.float32)
    hi = t.astype(ml_dtypes.bfloat16)
    lo = (t - hi.astype(np.float32)).astype(ml_dtypes.bfloat16)
    return hi, lo

def tables():
    k = np.arange(N)
    ang = 2*np.pi*((k[:,None]*k[None,:])%N)/N
    T = np.cos(ang)+np.sin(ang)
    hi, lo = split_np(T)
    wz = np.zeros((4,256,256), ml_dtypes.bfloat16)
    wi = np.zeros((4,256,256), ml_dtypes.bfloat16)
    for l in range(4):
        lane = (96*l + np.arange(N)) % 128
        wz[l, lane, 0:96] = hi
        wz[l, lane, 128:224] = lo
        wz[l, 128+lane, 0:96] = hi
        wi[l, 0:96, lane] = hi.T
        wi[l, 0:96, 128+lane] = lo.T
        wi[l, 128:224, lane] = hi.T
    def two(hi, lo):
        t = np.zeros((192,192), ml_dtypes.bfloat16)
        t[:96,:96]=hi; t[:96,96:]=hi; t[96:,:96]=lo
        return t
    order = np.array([4*kk+l for l in range(4) for kk in range(24)])
    ty = two(hi[:,order], lo[:,order])
    tyi = two(hi[order,:], lo[order,:])
    tx = two(hi, lo)
    return wz, wi, ty, tyi, tx

def kernel_table():
    idx = jnp.arange(N, dtype=jnp.int32)
    f = jnp.where(idx <= N//2, idx, idx-N).astype(jnp.float32)
    sq = f*f
    sqw = jnp.pad(sq, (0,32))
    g2 = (2.0*math.pi/CELL)**2 * (sq[:,None,None]+sq[None,:,None]+sqw[None,None,:])
    pos = g2 > 0
    safe = jnp.where(pos, g2, 1.0)
    val = 4.0*math.pi/safe * -jnp.expm1(-safe/(4.0*OMEGA*OMEGA))
    val = jnp.where(pos, val, math.pi/(OMEGA*OMEGA))
    return (val * (-0.25/float(N**3))).reshape(N*N, 128)

def split(x):
    hi = x.astype(bf)
    lo = (x - hi.astype(jnp.float32)).astype(bf)
    return hi, lo

def dot(a, b):
    return lax.dot_general(a, b, (((1,),(0,)),((),())), preferred_element_type=jnp.float32)

def left(t, x):
    hi, lo = split(x)
    q = dot(t, jnp.concatenate([hi, lo], axis=0))
    return q[:96] + q[96:]

def right(x, w):
    hi, lo = split(x)
    o = dot(jnp.concatenate([hi, lo], axis=1), w)
    return o[:, :128] + o[:, 128:]

def pair(i_ref, j_ref, near_ref, far_ref, a_ref, k_ref, wz_ref, wi_ref, ty_ref, tyi_ref, tx_ref, near_first, far_first, XB=8, VB=4, AS=96, stages=7):
    lane = lax.broadcasted_iota(jnp.int32, (24*XB, 128), 1)
    def fwd(xb, _):
        base = xb*(XB*72)
        d = []
        for s in range(3):
            rows = pl.ds(base+s, 24*XB, stride=3)
            d.append(i_ref[rows, :]*j_ref[rows, :])
        m = [d[0], jnp.where(lane >= 96, d[0], d[1]), jnp.where(lane >= 64, d[1], d[2]), d[2]]
        o = [right(m[l], wz_ref[l]) for l in range(4)]
        for xx in range(0, XB, 2):
            cols = []
            for x in (xx, xx+1):
                cols.append(jnp.concatenate([o[l][24*x:24*x+24] for l in range(4)], axis=0))
            q = left(ty_ref[...], jnp.concatenate(cols, axis=1))
            row = (xb*XB+xx)*AS
            a_ref[pl.ds(row, 96), :] = q[:, :128]
            a_ref[pl.ds(row+AS, 96), :] = q[:, 128:]
        return 0
    if stages & 1:
        lax.fori_loop(0, 96//XB, fwd, 0)
    def mid(vb, _):
        for vv in range(0, VB, 2):
            v = vb*VB+vv
            a = jnp.concatenate([a_ref[pl.ds(v, 96, stride=AS), :], a_ref[pl.ds(v+1, 96, stride=AS), :]], axis=1)
            kk = jnp.concatenate([k_ref[pl.ds(v*96, 96), :], k_ref[pl.ds(v*96+96, 96), :]], axis=1)
            b = left(tx_ref[...], left(tx_ref[...], a) * kk)
            a_ref[pl.ds(v, 96, stride=AS), :] = b[:, :128]
            a_ref[pl.ds(v+1, 96, stride=AS), :] = b[:, 128:]
        return 0
    if stages & 2:
        lax.fori_loop(0, 96//VB, mid, 0)
    def inv(xb, _):
        parts = [[] for _ in range(4)]
        for xx in range(0, XB, 2):
            row = (xb*XB+xx)*AS
            a = jnp.concatenate([a_ref[pl.ds(row, 96), :], a_ref[pl.ds(row+AS, 96), :]], axis=1)
            q = left(tyi_ref[...], a)
            for x in range(2):
                for l in range(4):
                    parts[l].append(q[24*l:24*l+24, 128*x:128*x+128])
        o = [right(jnp.concatenate(parts[l], axis=0), wi_ref[l]) for l in range(4)]
        vs = [jnp.where(lane < 96, o[0], o[1]), jnp.where(lane < 64, o[1], o[2]), jnp.where(lane < 32, o[2], o[3])]
        base = xb*(XB*72)
        for s in range(3):
            rows = pl.ds(base+s, 24*XB, stride=3)
            n = j_ref[rows, :]*vs[s]
            f = i_ref[rows, :]*vs[s]
            near_ref[rows, :] = n if near_first else near_ref[rows, :]+n
            far_ref[rows, :] = f if far_first else far_ref[rows, :]+f
        return 0
    if stages & 4:
        lax.fori_loop(0, 96//XB, inv, 0)


def exchange(i_hbm, j_hbm, k_ref, wz_ref, wi_ref, ty_ref, tyi_ref, tx_ref, near, far, iv, jv, nv, fv, a, sem):
    for g in range(2):
        pltpu.make_async_copy(i_hbm.at[g], iv.at[g], sem.at[g]).start()
        pltpu.make_async_copy(j_hbm.at[g], jv.at[g], sem.at[2 + g]).start()
    for g in range(2):
        pltpu.make_async_copy(i_hbm.at[g], iv.at[g], sem.at[g]).wait()
        pltpu.make_async_copy(j_hbm.at[g], jv.at[g], sem.at[2 + g]).wait()
    for gi, gj in ((0, 0), (0, 1), (1, 1), (1, 0)):
        pair(iv.at[gi], jv.at[gj], nv.at[gi], fv.at[gj], a, k_ref, wz_ref, wi_ref, ty_ref, tyi_ref, tx_ref,
             gj == gi, gi == 0, AS=97)
    for g in range(2):
        pltpu.make_async_copy(nv.at[g], near.at[g], sem.at[g]).start()
        pltpu.make_async_copy(fv.at[g], far.at[g], sem.at[2 + g]).start()
    for g in range(2):
        pltpu.make_async_copy(nv.at[g], near.at[g], sem.at[g]).wait()
        pltpu.make_async_copy(fv.at[g], far.at[g], sem.at[2 + g]).wait()


def run_pairs(i, j):
    grid = jax.ShapeDtypeStruct((2, 6912, 128), jnp.float32)
    vm = pl.BlockSpec(memory_space=pltpu.VMEM)
    an = pl.BlockSpec(memory_space=pl.ANY)
    return pl.pallas_call(
        exchange,
        out_shape=[grid, grid],
        in_specs=[an, an] + [vm] * 6,
        out_specs=[an, an],
        scratch_shapes=[pltpu.VMEM((2, 6912, 128), jnp.float32)] * 4
        + [pltpu.VMEM((96 * 97, 128), jnp.float32), pltpu.SemaphoreType.DMA((4,))],
        compiler_params=pltpu.CompilerParams(vmem_limit_bytes=62 * 1024 * 1024),
    )(i, j, kernel_table(), *tables())


def local(orbitals):
    own = orbitals.reshape(8, 6, 72, 128)
    mine = lax.all_to_all(own.reshape(4, 2, 6, 72, 128), ("zl", "c"), 0, 0)
    mine = lax.all_gather(mine, "x").reshape(4, 2, 2, 2, 6, 72, 128)
    i = mine.transpose(3, 1, 0, 2, 4, 5, 6).reshape(2, 6912, 128)
    partners = lax.all_gather(own[0:2], ("y", "zh"))[0:4]
    partners = lax.all_to_all(partners, "x", 0, 0)
    partners = lax.all_gather(partners, ("zl", "c")).reshape(2, 2, 4, 2, 6, 72, 128)
    j = partners.transpose(3, 0, 2, 1, 4, 5, 6).reshape(2, 6912, 128)
    near, far = run_pairs(i, j)
    near = near.reshape(2, 2, 4, 2, 6, 72, 128).transpose(2, 1, 3, 0, 4, 5, 6)
    near = lax.psum_scatter(near, "x", scatter_dimension=0).reshape(4, 2, 6, 72, 128)
    near = lax.all_to_all(near, ("zl", "c"), 0, 0).reshape(8, 6, 72, 128)
    far = far.reshape(2, 2, 4, 2, 6, 72, 128).transpose(1, 3, 2, 0, 4, 5, 6).reshape(4, 4, 2, 6, 72, 128)
    far = lax.psum_scatter(far, ("zl", "c"), scatter_dimension=0)
    far = lax.all_to_all(far, "x", 0, 0)
    far = lax.psum(far, ("y", "zh"))
    band = lax.axis_index(("y", "zh"))
    extra = sum(jnp.where(band == r, far[r], 0.0) for r in range(4))
    out = near.at[0:2].add(extra)
    return out.reshape(8, 6, 9216)


def solution(mesh):
    fine = jax.sharding.Mesh(mesh.devices.reshape(4, 2, 2, 4, 2), ("y", "zh", "zl", "x", "c"))
    placed = P(("y", "zh"), ("zl", "x", "c"), None)
    return jax.shard_map(local, mesh=fine, in_specs=(placed,), out_specs=placed, check_vma=False)
```

```python
import math, functools
import numpy as np
import jax, jax.numpy as jnp
from jax import lax
from jax.experimental import pallas as pl
from jax.experimental.pallas import tpu as pltpu
from jax.sharding import PartitionSpec as P
import ml_dtypes

N = 96
OMEGA = 0.106
CELL = 41.05
bf = jnp.bfloat16

def split_np(t):
    t = t.astype(np.float32)
    hi = t.astype(ml_dtypes.bfloat16)
    lo = (t - hi.astype(np.float32)).astype(ml_dtypes.bfloat16)
    return hi, lo

def tables():
    k = np.arange(N)
    ang = 2*np.pi*((k[:,None]*k[None,:])%N)/N
    T = np.cos(ang)+np.sin(ang)
    hi, lo = split_np(T)
    wz = np.zeros((4,256,256), ml_dtypes.bfloat16)
    wi = np.zeros((4,256,256), ml_dtypes.bfloat16)
    for l in range(4):
        lane = (96*l + np.arange(N)) % 128
        wz[l, lane, 0:96] = hi
        wz[l, lane, 128:224] = lo
        wz[l, 128+lane, 0:96] = hi
        wi[l, 0:96, lane] = hi.T
        wi[l, 0:96, 128+lane] = lo.T
        wi[l, 128:224, lane] = hi.T
    def two(hi, lo):
        t = np.zeros((192,192), ml_dtypes.bfloat16)
        t[:96,:96]=hi; t[:96,96:]=hi; t[96:,:96]=lo
        return t
    order = np.array([4*kk+l for l in range(4) for kk in range(24)])
    ty = two(hi[:,order], lo[:,order])
    tyi = two(hi[order,:], lo[order,:])
    tx = two(hi, lo)
    return wz, wi, ty, tyi, tx

def kernel_table():
    idx = jnp.arange(N, dtype=jnp.int32)
    f = jnp.where(idx <= N//2, idx, idx-N).astype(jnp.float32)
    sq = f*f
    sqw = jnp.pad(sq, (0,32))
    g2 = (2.0*math.pi/CELL)**2 * (sq[:,None,None]+sq[None,:,None]+sqw[None,None,:])
    pos = g2 > 0
    safe = jnp.where(pos, g2, 1.0)
    val = 4.0*math.pi/safe * -jnp.expm1(-safe/(4.0*OMEGA*OMEGA))
    val = jnp.where(pos, val, math.pi/(OMEGA*OMEGA))
    return (val * (-0.25/float(N**3))).reshape(N*N, 128)

def split(x):
    hi = x.astype(bf)
    lo = (x - hi.astype(jnp.float32)).astype(bf)
    return hi, lo

def dot(a, b):
    return lax.dot_general(a, b, (((1,),(0,)),((),())), preferred_element_type=jnp.float32)

def left(t, x):
    hi, lo = split(x)
    q = dot(t, jnp.concatenate([hi, lo], axis=0))
    return q[:96] + q[96:]

def right(x, w):
    hi, lo = split(x)
    o = dot(jnp.concatenate([hi, lo], axis=1), w)
    return o[:, :128] + o[:, 128:]

def pair(i_ref, j_ref, near_ref, far_ref, a_ref, k_ref, wz_ref, wi_ref, ty_ref, tyi_ref, tx_ref, near_first, far_first, XB=8, VB=4, AS=96, stages=7, hooks=None):
    lane = lax.broadcasted_iota(jnp.int32, (24*XB, 128), 1)
    def fwd(xb, _):
        base = xb*(XB*72)
        d = []
        for s in range(3):
            rows = pl.ds(base+s, 24*XB, stride=3)
            d.append(i_ref[rows, :]*j_ref[rows, :])
        m = [d[0], jnp.where(lane >= 96, d[0], d[1]), jnp.where(lane >= 64, d[1], d[2]), d[2]]
        o = [right(m[l], wz_ref[l]) for l in range(4)]
        for xx in range(0, XB, 2):
            cols = []
            for x in (xx, xx+1):
                cols.append(jnp.concatenate([o[l][24*x:24*x+24] for l in range(4)], axis=0))
            q = left(ty_ref[...], jnp.concatenate(cols, axis=1))
            row = (xb*XB+xx)*AS
            a_ref[pl.ds(row, 96), :] = q[:, :128]
            a_ref[pl.ds(row+AS, 96), :] = q[:, 128:]
        return 0
    if stages & 1:
        lax.fori_loop(0, 96//XB, fwd, 0)
    if hooks:
        hooks[0]()
    def mid(vb, _):
        for vv in range(0, VB, 2):
            v = vb*VB+vv
            a = jnp.concatenate([a_ref[pl.ds(v, 96, stride=AS), :], a_ref[pl.ds(v+1, 96, stride=AS), :]], axis=1)
            kk = jnp.concatenate([k_ref[pl.ds(v*96, 96), :], k_ref[pl.ds(v*96+96, 96), :]], axis=1)
            b = left(tx_ref[...], left(tx_ref[...], a) * kk)
            a_ref[pl.ds(v, 96, stride=AS), :] = b[:, :128]
            a_ref[pl.ds(v+1, 96, stride=AS), :] = b[:, 128:]
        return 0
    if stages & 2:
        lax.fori_loop(0, 96//VB, mid, 0)
    if hooks:
        hooks[1]()
    def inv(xb, _):
        parts = [[] for _ in range(4)]
        for xx in range(0, XB, 2):
            row = (xb*XB+xx)*AS
            a = jnp.concatenate([a_ref[pl.ds(row, 96), :], a_ref[pl.ds(row+AS, 96), :]], axis=1)
            q = left(tyi_ref[...], a)
            for x in range(2):
                for l in range(4):
                    parts[l].append(q[24*l:24*l+24, 128*x:128*x+128])
        o = [right(jnp.concatenate(parts[l], axis=0), wi_ref[l]) for l in range(4)]
        vs = [jnp.where(lane < 96, o[0], o[1]), jnp.where(lane < 64, o[1], o[2]), jnp.where(lane < 32, o[2], o[3])]
        base = xb*(XB*72)
        for s in range(3):
            rows = pl.ds(base+s, 24*XB, stride=3)
            n = j_ref[rows, :]*vs[s]
            f = i_ref[rows, :]*vs[s]
            near_ref[rows, :] = n if near_first else near_ref[rows, :]+n
            far_ref[rows, :] = f if far_first else far_ref[rows, :]+f
        return 0
    if stages & 4:
        lax.fori_loop(0, 96//XB, inv, 0)


MESH = pl.DeviceIdType.MESH
PIECE = 432


class Comm:
    def __init__(self, ss, rs):
        self.ss, self.rs, self.sent, self.n, self.r = ss, rs, [], 0, 0

    def slot(self, count=1):
        self.r += count
        return self.r - count

    def send(self, src, dst, recv, device, when=None):
        copy = pltpu.make_async_remote_copy(src_ref=src, dst_ref=dst, send_sem=self.ss.at[self.n], recv_sem=self.rs.at[recv],
                                            device_id=device, device_id_type=MESH)
        self.n += 1
        self.sent.append((copy, when))
        guarded(when, copy.start)

    def wait(self, ref, recv):
        pltpu.make_async_copy(ref, ref, self.rs.at[recv]).wait()

    def finish(self):
        for copy, when in self.sent:
            guarded(when, copy.wait_send)


def guarded(when, do):
    if when is None:
        do()
    else:
        pl.when(when)(lambda: do())


def piece(zl, x, c):
    return pl.ds(pl.multiple_of((zl * 8 + x * 2 + c) * PIECE, PIECE), PIECE)


def exchange(o, k_ref, wz_ref, wi_ref, ty_ref, tyi_ref, tx_ref, out, extra, iv, jv, nv, fv, a, fw, rb, db, zb, zc, yb, ss, rs, ls):
    y, zh, zl, x, c = (lax.axis_index(n) for n in ("y", "zh", "zl", "x", "c"))
    xs = [lax.rem(x + d, 4) for d in range(4)]
    ys = [lax.rem(y + d, 4) for d in range(4)]
    own = 2 * zl + c
    quad = [(zl if k < 2 else 1 - zl, c if k % 2 == 0 else 1 - c) for k in range(4)]
    in_root_zh = zh == lax.rem(x, 2)
    off_root_zh = jnp.logical_not(in_root_zh)
    dy = lax.rem(y + 4 - lax.div(x, 2), 4)
    root = in_root_zh & (dy == 0)
    branch = in_root_zh & (dy != 0)
    prim = jnp.where(in_root_zh, zl, 1 - zl)
    band = 2 * y + zh
    gives = y < 2
    dx_root = lax.rem(x + 8 - band, 4)

    def at(y=y, zh=zh, zl=zl, x=x, c=c):
        return (y, zh, zl, x, c)

    barrier = pltpu.get_barrier_semaphore()
    zn = (1 - zh, 1 - zl)
    friends = [at(x=xs[1]), at(x=xs[2]), at(x=xs[3]), at(y=ys[1]), at(y=ys[3]), at(zh=zn[0], zl=zn[1])]
    friends += [at(zl=qz, c=qc) for qz, qc in quad[1:]]
    for f in friends:
        pl.semaphore_signal(barrier, inc=1, device_id=f, device_id_type=MESH)
    pl.semaphore_wait(barrier, len(friends))

    m = Comm(ss, rs)
    S1 = [[m.slot() for _ in range(4)] for _ in range(2)]
    S2 = [[[m.slot() for _ in range(4)] for _ in range(2)] for _ in range(2)]
    S3 = [[[m.slot() for _ in range(2)] for _ in range(2)] for _ in range(2)]
    J1 = [m.slot(4) for _ in range(2)]
    YM, ZAB, SEC = ([[m.slot() for _ in range(4)] for _ in range(2)] for _ in range(3))
    DIE = [[[m.slot() for _ in range(4)] for _ in range(2)] for _ in range(2)]
    keep = [pltpu.make_async_copy(o.at[2 * own + g], iv.at[g, piece(zl, x, c)], ls.at[g]) for g in range(2)]
    root_keep = [pltpu.make_async_copy(o.at[g], jv.at[g, piece(zl, x, c)], ls.at[2 + g]) for g in range(2)]

    def i_first(g):
        for k in range(1, 4):
            qz, qc = quad[k]
            m.send(o.at[2 * (2 * qz + qc) + g], iv.at[g, piece(zl, x, c)], S1[g][k], at(zl=qz, c=qc))
        keep[g].start()

    def i_spread(g, k):
        rows = piece(quad[k][0], x, quad[k][1])
        src = iv.at[g, rows]
        if k == 0:
            src = o.at[2 * own + g]
        else:
            m.wait(src, S1[g][k])
        for d in range(2):
            m.send(src, iv.at[g, rows], S2[g][d][k], at(x=xs[1 + 2 * d]))

    def i_forward(g):
        for kk in range(2):
            for d in range(2):
                k = kk + 2 * d
                rows = iv.at[g, piece(quad[k][0], xs[3 - 2 * d], quad[k][1])]
                m.wait(rows, S2[g][d][k])
                m.send(rows, rows, S3[g][d][kk], at(x=xs[1 + 2 * d]))

    def i_finish(g):
        keep[g].wait()
        rows = iv.at[g, pl.ds(0, PIECE)]
        for d in range(2):
            for kk in range(2):
                m.wait(rows, S2[g][d][kk + 2 - 2 * d])
                m.wait(rows, S3[g][d][kk])

    def j_first(g):
        m.send(o.at[g], jv.at[g, piece(zl, x, c)], J1[g] + dx_root, at(x=band), gives & (dx_root != 0))
        guarded(root, root_keep[g].start)

    def j_primary(g):
        for dx in range(4):
            rows = jv.at[g, piece(prim, xs[dx], c)]
            guarded(root, root_keep[g].wait if dx == 0 else lambda: m.wait(rows, J1[g] + dx))
            guarded(branch, lambda: m.wait(rows, YM[g][dx]))
            guarded(off_root_zh, lambda: m.wait(rows, ZAB[g][dx]))
            m.send(rows, rows, YM[g][dx], at(y=ys[1]), root | (branch & (dy == 1)) if dx < 2 else root)
            m.send(rows, rows, YM[g][dx], at(y=ys[3]), root | (branch & (dy == 3)) if dx >= 2 else root)
            m.send(rows, rows, ZAB[g][dx], at(zh=zn[0], zl=zn[1]), in_root_zh)
            m.send(rows, rows, SEC[g][dx], at(zl=1 - zl))
            m.send(rows, rows, DIE[g][0][dx], at(c=1 - c))

    def j_secondary(g):
        for dx in range(4):
            rows = jv.at[g, piece(1 - prim, xs[dx], c)]
            m.wait(rows, SEC[g][dx])
            m.send(rows, rows, DIE[g][1][dx], at(c=1 - c))

    def j_finish(g):
        for s in range(2):
            for dx in range(4):
                m.wait(jv.at[g, pl.ds(0, PIECE)], DIE[g][s][dx])

    R1 = [[[m.slot() for _ in range(2)] for _ in range(2)] for _ in range(2)]
    R2 = [[[m.slot() for _ in range(4)] for _ in range(2)] for _ in range(2)]
    R4 = [[m.slot() for _ in range(4)] for _ in range(2)]
    put = [pltpu.make_async_copy(nv.at[g, piece(zl, x, c)], out.at[2 * own + g], ls.at[4 + g]) for g in range(2)]

    def n_first(g):
        for kk in range(2):
            for d in range(2):
                k = kk + 2 * d
                m.send(nv.at[g, piece(quad[k][0], xs[2], quad[k][1])], fw.at[g, d, kk], R1[g][d][kk], at(x=xs[1 + 2 * d]))
        for kk in range(2):
            for d in range(2):
                k = kk + 2 - 2 * d
                rows = nv.at[g, piece(quad[k][0], xs[1 + 2 * d], quad[k][1])]
                m.send(rows, rows_of(rb, g, d, k), R2[g][d][k], at(x=xs[1 + 2 * d]))

    def rows_of(ref, *index):
        return ref.at[index]

    def n_second(g):
        for kk in range(2):
            for d in range(2):
                k = kk + 2 * d
                m.wait(fw.at[g, d, kk], R1[g][d][kk])
                rows = nv.at[g, piece(quad[k][0], xs[1 + 2 * d], quad[k][1])]
                rows[...] += fw[g, d, kk]
                m.send(rows, rb.at[g, d, k], R2[g][d][k], at(x=xs[1 + 2 * d]))

    def n_third(g):
        for k in (1, 2, 3, 0):
            rows = nv.at[g, piece(quad[k][0], x, quad[k][1])]
            m.wait(rb.at[g, 0, k], R2[g][0][k])
            m.wait(rb.at[g, 1, k], R2[g][1][k])
            rows[...] += rb[g, 0, k] + rb[g, 1, k]
            if k == 0:
                put[g].start()
            else:
                m.send(rows, out.at[2 * own + g], R4[g][k], at(zl=quad[k][0], c=quad[k][1]))

    def n_finish(g):
        for k in range(1, 4):
            m.wait(out.at[g], R4[g][k])
        put[g].wait()

    D1 = [[[m.slot() for _ in range(4)] for _ in range(2)] for _ in range(2)]
    D2, D3 = ([[m.slot() for _ in range(4)] for _ in range(2)] for _ in range(2))
    D4 = [[[m.slot() for _ in range(4)] for _ in range(2)] for _ in range(2)]
    D5 = [m.slot() for _ in range(2)]
    root_put = [pltpu.make_async_copy(fv.at[g, piece(zl, x, c)], extra.at[g], ls.at[6 + g]) for g in range(2)]

    def f_first(g):
        for s in (1, 0):
            for dx in range(4):
                m.send(fv.at[g, piece(prim if s == 0 else 1 - prim, xs[dx], 1 - c)], db.at[g, s, dx], D1[g][s][dx], at(c=1 - c))

    def f_second(g):
        for dx in range(4):
            rows = fv.at[g, piece(1 - prim, xs[dx], c)]
            m.wait(db.at[g, 1, dx], D1[g][1][dx])
            rows[...] += db[g, 1, dx]
            m.send(rows, zb.at[g, dx], D2[g][dx], at(zl=1 - zl))

    def f_third(g):
        for dx in range(4):
            rows = fv.at[g, piece(prim, xs[dx], c)]
            m.wait(db.at[g, 0, dx], D1[g][0][dx])
            m.wait(zb.at[g, dx], D2[g][dx])
            rows[...] += db[g, 0, dx] + zb[g, dx]
            m.send(rows, zc.at[g, dx], D3[g][dx], at(zh=zn[0], zl=zn[1]), off_root_zh)

    def f_fourth(g):
        for dx in (0, 2, 1, 3):
            rows = fv.at[g, piece(prim, xs[dx], c)]

            def add(ref, slot):
                m.wait(ref, slot)
                rows[...] += ref[...]

            near_y, far_y = (0, 1) if dx < 2 else (1, 0)
            guarded(in_root_zh, lambda: add(zc.at[g, dx], D3[g][dx]))
            m.send(rows, yb.at[g, near_y, dx], D4[g][near_y][dx], at(y=ys[3 - 2 * near_y]), in_root_zh & (dy == 2))

    def f_fifth(g):
        for dx in (0, 2, 1, 3):
            rows = fv.at[g, piece(prim, xs[dx], c)]

            def add(ref, slot):
                m.wait(ref, slot)
                rows[...] += ref[...]

            near_y = 0 if dx < 2 else 1
            guarded(in_root_zh & (dy == 1 + 2 * near_y), lambda: add(yb.at[g, near_y, dx], D4[g][near_y][dx]))
            for e in range(2):
                m.send(rows, yb.at[g, e, dx], D4[g][e][dx], at(y=ys[3 - 2 * e]), in_root_zh & (dy == 1 + 2 * e))

    def f_sixth(g):
        for dx in (0, 2, 1, 3):
            rows = fv.at[g, piece(prim, xs[dx], c)]

            def add():
                for e in range(2):
                    m.wait(yb.at[g, e, dx], D4[g][e][dx])
                rows[...] += yb[g, 0, dx] + yb[g, 1, dx]

            guarded(root, add)
            if dx == 0:
                guarded(root, root_put[g].start)
            else:
                m.send(rows, extra.at[g], D5[g], at(x=xs[dx]), root)

    def f_finish(g):
        guarded(gives & (dx_root != 0), lambda: m.wait(extra.at[g], D5[g]))
        guarded(root, root_put[g].wait)

    def work(gi, gj, first, second):
        pair(iv.at[gi], jv.at[gj], nv.at[gi], fv.at[gj], a, k_ref, wz_ref, wi_ref, ty_ref, tyi_ref, tx_ref, gj == gi, gi == 0,
             AS=97, hooks=(first, second))

    i_first(0)
    i_spread(0, 0)
    j_first(0)
    i_first(1)
    j_first(1)
    for k in range(1, 4):
        i_spread(0, k)
    i_spread(1, 0)
    j_primary(0)
    i_forward(0)
    for k in range(1, 4):
        i_spread(1, k)
    j_secondary(0)
    j_primary(1)
    i_finish(0)
    j_finish(0)

    def in_first():
        i_forward(1)
        j_secondary(1)

    work(0, 0, in_first, lambda: None)
    j_finish(1)
    work(0, 1, lambda: None, lambda: None)
    n_first(0)
    i_finish(1)
    work(1, 1, lambda: n_second(0), lambda: n_third(0))
    f_first(1)

    def far_a():
        f_second(1)
        f_third(1)

    def far_b():
        f_fourth(1)
        f_fifth(1)

    work(1, 0, far_a, far_b)
    n_first(1)
    f_first(0)
    n_second(1)
    f_second(0)
    f_third(0)
    n_third(1)
    f_fourth(0)
    f_fifth(0)
    f_sixth(1)
    f_sixth(0)
    for g in range(2):
        n_finish(g)
        f_finish(g)
    m.finish()


SENDS, RECEIVES = 256, 256


def run_pairs(own):
    vm = pl.BlockSpec(memory_space=pltpu.VMEM)
    an = pl.BlockSpec(memory_space=pl.ANY)
    f32 = jnp.float32
    big = pltpu.VMEM((2, 6912, 128), f32)

    def pieces(*lead):
        return pltpu.VMEM(lead + (PIECE, 128), f32)

    return pl.pallas_call(
        exchange,
        out_shape=[jax.ShapeDtypeStruct((8, PIECE, 128), f32), jax.ShapeDtypeStruct((2, PIECE, 128), f32)],
        in_specs=[an] + [vm] * 6,
        out_specs=[an, an],
        scratch_shapes=[big] * 4
        + [pltpu.VMEM((96 * 97, 128), f32), pieces(2, 2, 2), pieces(2, 2, 4), pieces(2, 2, 4), pieces(2, 4), pieces(2, 4), pieces(2, 2, 4)]
        + [pltpu.SemaphoreType.DMA((SENDS,)), pltpu.SemaphoreType.DMA((RECEIVES,)), pltpu.SemaphoreType.DMA((8,))],
        compiler_params=pltpu.CompilerParams(vmem_limit_bytes=67043328, collective_id=1, has_side_effects=True),
    )(own, kernel_table(), *tables())


def local(orbitals):
    own = orbitals.reshape(8, PIECE, 128)
    near, far = run_pairs(own)
    gives = lax.axis_index("y") < 2
    out = near.at[0:2].add(jnp.where(gives, far, 0.0))
    return out.reshape(8, 6, 9216)


def solution(mesh):
    fine = jax.sharding.Mesh(mesh.devices.reshape(4, 2, 2, 4, 2), ("y", "zh", "zl", "x", "c"))
    placed = P(("y", "zh"), ("zl", "x", "c"), None)
    return jax.shard_map(local, mesh=fine, in_specs=(placed,), out_specs=placed, check_vma=False)
```

```python
import math, functools
import numpy as np
import jax, jax.numpy as jnp
from jax import lax
from jax.experimental import pallas as pl
from jax.experimental.pallas import tpu as pltpu
from jax.sharding import PartitionSpec as P
import ml_dtypes

N = 96
OMEGA = 0.106
CELL = 41.05
bf = jnp.bfloat16
XB, VB, AS = 24, 24, 97

def split_np(t):
    t = t.astype(np.float32)
    hi = t.astype(ml_dtypes.bfloat16)
    lo = (t - hi.astype(np.float32)).astype(ml_dtypes.bfloat16)
    return hi, lo

def tables():
    k = np.arange(N)
    ang = 2*np.pi*((k[:,None]*k[None,:])%N)/N
    T = np.cos(ang)+np.sin(ang)
    hi, lo = split_np(T)
    wz = np.zeros((4,256,256), ml_dtypes.bfloat16)
    wi = np.zeros((4,256,256), ml_dtypes.bfloat16)
    for l in range(4):
        lane = (96*l + np.arange(N)) % 128
        wz[l, lane, 0:96] = hi
        wz[l, lane, 128:224] = lo
        wz[l, 128+lane, 0:96] = hi
        wi[l, 0:96, lane] = hi.T
        wi[l, 0:96, 128+lane] = lo.T
        wi[l, 128:224, lane] = hi.T
    def two(hi, lo):
        t = np.zeros((192,192), ml_dtypes.bfloat16)
        t[:96,:96]=hi; t[:96,96:]=hi; t[96:,:96]=lo
        return t
    order = np.array([4*kk+l for l in range(4) for kk in range(24)])
    ty = two(hi[:,order], lo[:,order])
    tyi = two(hi[order,:], lo[order,:])
    tx = two(hi, lo)
    return wz, wi, ty, tyi, tx

def kernel_table():
    idx = jnp.arange(N, dtype=jnp.int32)
    f = jnp.where(idx <= N//2, idx, idx-N).astype(jnp.float32)
    sq = f*f
    sqw = jnp.pad(sq, (0,32))
    g2 = (2.0*math.pi/CELL)**2 * (sq[:,None,None]+sq[None,:,None]+sqw[None,None,:])
    pos = g2 > 0
    safe = jnp.where(pos, g2, 1.0)
    val = 4.0*math.pi/safe * -jnp.expm1(-safe/(4.0*OMEGA*OMEGA))
    val = jnp.where(pos, val, math.pi/(OMEGA*OMEGA))
    return (val * (-0.25/float(N**3))).reshape(N*N, 128)

def split(x):
    hi = x.astype(bf)
    lo = (x - hi.astype(jnp.float32)).astype(bf)
    return hi, lo

def dot(a, b):
    return lax.dot_general(a, b, (((1,),(0,)),((),())), preferred_element_type=jnp.float32)

def left(t, x):
    hi, lo = split(x)
    q = dot(t, jnp.concatenate([hi, lo], axis=0))
    return q[:96] + q[96:]

def right(x, w):
    hi, lo = split(x)
    o = dot(jnp.concatenate([hi, lo], axis=1), w)
    return o[:, :128] + o[:, 128:]


def transform_pairs(iv, jv, nv, fv, a_ref, k_ref, wz_ref, wi_ref, ty_ref, tyi_ref, tx_ref, point):
    lane = lax.broadcasted_iota(jnp.int32, (24 * XB, 128), 1)

    def one(t, _):
        gi = t // 2
        gj = ((t + 1) // 2) % 2
        i_ref, j_ref, near_ref, far_ref = iv.at[gi], jv.at[gj], nv.at[gi], fv.at[gj]
        near_first, far_first = gi == gj, gi == 0
        point(t, 0)

        def fwd(xb, _):
            base = xb * (XB * 72)
            d = []
            for s in range(3):
                rows = pl.ds(base + s, 24 * XB, stride=3)
                d.append(i_ref[rows, :] * j_ref[rows, :])
            m = [d[0], jnp.where(lane >= 96, d[0], d[1]), jnp.where(lane >= 64, d[1], d[2]), d[2]]
            o = [right(m[l], wz_ref[l]) for l in range(4)]
            for xx in range(0, XB, 2):
                cols = []
                for x in (xx, xx + 1):
                    cols.append(jnp.concatenate([o[l][24 * x:24 * x + 24] for l in range(4)], axis=0))
                q = left(ty_ref[...], jnp.concatenate(cols, axis=1))
                row = (xb * XB + xx) * AS
                a_ref[pl.ds(row, 96), :] = q[:, :128]
                a_ref[pl.ds(row + AS, 96), :] = q[:, 128:]
            return 0

        lax.fori_loop(0, 96 // XB, fwd, 0)
        point(t, 1)

        def mid(vb, _):
            for vv in range(0, VB, 2):
                v = vb * VB + vv
                b = jnp.concatenate([a_ref[pl.ds(v, 96, stride=AS), :], a_ref[pl.ds(v + 1, 96, stride=AS), :]], axis=1)
                kk = jnp.concatenate([k_ref[pl.ds(v * 96, 96), :], k_ref[pl.ds(v * 96 + 96, 96), :]], axis=1)
                b = left(tx_ref[...], left(tx_ref[...], b) * kk)
                a_ref[pl.ds(v, 96, stride=AS), :] = b[:, :128]
                a_ref[pl.ds(v + 1, 96, stride=AS), :] = b[:, 128:]
            return 0

        lax.fori_loop(0, 96 // VB, mid, 0)
        point(t, 2)

        def inv(xb, _):
            parts = [[] for _ in range(4)]
            for xx in range(0, XB, 2):
                row = (xb * XB + xx) * AS
                b = jnp.concatenate([a_ref[pl.ds(row, 96), :], a_ref[pl.ds(row + AS, 96), :]], axis=1)
                q = left(tyi_ref[...], b)
                for x in range(2):
                    for l in range(4):
                        parts[l].append(q[24 * l:24 * l + 24, 128 * x:128 * x + 128])
            o = [right(jnp.concatenate(parts[l], axis=0), wi_ref[l]) for l in range(4)]
            vs = [jnp.where(lane < 96, o[0], o[1]), jnp.where(lane < 64, o[1], o[2]), jnp.where(lane < 32, o[2], o[3])]
            base = xb * (XB * 72)
            for s in range(3):
                rows = pl.ds(base + s, 24 * XB, stride=3)
                near_ref[rows, :] = jnp.where(near_first, 0.0, near_ref[rows, :]) + j_ref[rows, :] * vs[s]
                far_ref[rows, :] = jnp.where(far_first, 0.0, far_ref[rows, :]) + i_ref[rows, :] * vs[s]
            return 0

        lax.fori_loop(0, 96 // XB, inv, 0)
        return 0

    lax.fori_loop(0, 4, one, 0)


MESH = pl.DeviceIdType.MESH
PIECE = 432


class Comm:
    def __init__(self, ss, rs, some):
        self.ss, self.rs, self.some, self.sent, self.n, self.r = ss, rs, some, [], 0, 0

    def slot(self):
        self.r += 1
        return self.r - 1

    def send(self, src, dst, recv, device, when=None):
        copy = pltpu.make_async_remote_copy(src_ref=src, dst_ref=dst, send_sem=self.ss.at[self.n], recv_sem=self.rs.at[recv],
                                            device_id=device, device_id_type=MESH)
        self.n += 1
        self.sent.append(when)
        guarded(when, copy.start)

    def wait(self, recv):
        pltpu.make_async_copy(self.some, self.some, self.rs.at[recv]).wait()

    def finish(self):
        for n, when in enumerate(self.sent):
            guarded(when, pltpu.make_async_copy(self.some, self.some, self.ss.at[n]).wait)


def guarded(when, do):
    if when is None:
        do()
    else:
        pl.when(when)(lambda: do())


def piece(zl, x, c):
    return pl.ds(pl.multiple_of((zl * 8 + x * 2 + c) * PIECE, PIECE), PIECE)


def exchange(o, k_ref, wz_ref, wi_ref, ty_ref, tyi_ref, tx_ref, out, extra, iv, jv, nv, fv, a, fw, rb, db, zb, zc, yb, ss, rs, ls):
    y, zh, zl, x, c = (lax.axis_index(n) for n in ("y", "zh", "zl", "x", "c"))
    xs = [lax.rem(x + d, 4) for d in range(4)]
    ys = [lax.rem(y + d, 4) for d in range(4)]
    own = 2 * zl + c
    quad = [(zl if k < 2 else 1 - zl, c if k % 2 == 0 else 1 - c) for k in range(4)]
    root_y, root_zh = lax.div(x, 2), lax.rem(x, 2)
    dy = lax.rem(y + 4 - root_y, 4)
    in_root_zh = zh == root_zh
    home = [in_root_zh, jnp.logical_not(in_root_zh)]
    away = [home[1], home[0]]
    prim = jnp.where(in_root_zh, zl, 1 - zl)
    band = 2 * y + zh
    gives = y < 2
    shift = lax.rem(x + 8 - band, 4)
    units = [lax.rem(x + dy + j, 4) for j in range(4)]

    def at(y=y, zh=zh, zl=zl, x=x, c=c):
        return (y, zh, zl, x, c)

    entry = [at(x=lax.rem(band, 4), y=lax.rem(y + shift, 4)), at(x=lax.rem(band, 4), y=lax.rem(y + shift, 4), zh=1 - zh, zl=1 - zl)]
    source = at(x=units[0], y=root_y, zh=root_zh, zl=prim)
    at_home_0 = jnp.logical_and(in_root_zh, dy == 0)
    gives_away = [jnp.logical_and(gives, shift != 0), gives]
    takes = [jnp.logical_and(in_root_zh, dy != 0), home[1]]
    gets = jnp.logical_not(at_home_0)

    barrier = pltpu.get_barrier_semaphore()
    cross = at(zh=1 - zh, zl=1 - zl)
    friends = [at(x=xs[1]), at(x=xs[2]), at(x=xs[3]), at(y=ys[1]), at(y=ys[3]), cross]
    friends += [at(zl=qz, c=qc) for qz, qc in quad[1:]]
    for f in friends:
        pl.semaphore_signal(barrier, inc=1, device_id=f, device_id_type=MESH)
    for g in range(2):
        guarded(gives_away[g], lambda: pl.semaphore_signal(barrier, inc=1, device_id=entry[g], device_id_type=MESH))
    guarded(gets, lambda: pl.semaphore_signal(barrier, inc=1, device_id=source, device_id_type=MESH))
    count = gets.astype(jnp.int32) + gives_away[0].astype(jnp.int32) + gives_away[1].astype(jnp.int32)
    pl.semaphore_wait(barrier, len(friends) + count)

    m = Comm(ss, rs, fw.at[0, 0, 0])

    def slots(*shape):
        return [slots(*shape[1:]) for _ in range(shape[0])] if shape else m.slot()

    S1, S2, S3 = slots(2, 4), slots(2, 2, 4), slots(2, 2, 2)
    J1, YM, ZAB, SEC, DIE = slots(2), slots(2, 4), slots(2, 4), slots(2, 4), slots(2, 2, 4)
    keep = [pltpu.make_async_copy(o.at[2 * own + g], iv.at[g, piece(zl, x, c)], ls.at[g]) for g in range(2)]
    root_keep = pltpu.make_async_copy(o.at[0], jv.at[0, piece(zl, x, c)], ls.at[2])

    def i_first(g):
        for k in range(1, 4):
            qz, qc = quad[k]
            m.send(o.at[2 * (2 * qz + qc) + g], iv.at[g, piece(zl, x, c)], S1[g][k], at(zl=qz, c=qc))
        keep[g].start()

    def i_spread(g, k):
        rows = piece(quad[k][0], x, quad[k][1])
        src = iv.at[g, rows]
        if k == 0:
            src = o.at[2 * own + g]
        else:
            m.wait(S1[g][k])
        for d in range(2):
            m.send(src, iv.at[g, rows], S2[g][d][k], at(x=xs[1 + 2 * d]))

    def i_forward(g):
        for kk in range(2):
            for d in range(2):
                k = kk + 2 * d
                rows = iv.at[g, piece(quad[k][0], xs[3 - 2 * d], quad[k][1])]
                m.wait(S2[g][d][k])
                m.send(rows, rows, S3[g][d][kk], at(x=xs[1 + 2 * d]))

    def i_finish(g):
        keep[g].wait()
        for d in range(2):
            for kk in range(2):
                m.wait(S2[g][d][kk + 2 - 2 * d])
                m.wait(S3[g][d][kk])

    def j_first(g):
        m.send(o.at[g], jv.at[g, piece(zl, x, c)], J1[g], entry[g], gives_away[g])
        if g == 0:
            guarded(at_home_0, root_keep.start)

    def j_step(g, j):
        rows = jv.at[g, piece(prim, units[j], c)]
        if j == 0:
            if g == 0:
                guarded(at_home_0, root_keep.wait)
            guarded(takes[g], lambda: m.wait(J1[g]))
            for d in range(2):
                m.send(rows, rows, YM[g][3 - 2 * d], at(y=ys[1 + 2 * d]), home[g])
        else:
            guarded(home[g], lambda: m.wait(YM[g][j]))
            if (g, j) in ((0, 3), (1, 1)):
                m.send(rows, rows, YM[g][2], at(y=ys[1 + 2 * g]), home[g])
        guarded(away[g], lambda: m.wait(ZAB[g][j]))
        m.send(rows, rows, ZAB[g][j], cross, home[g])
        m.send(rows, rows, SEC[g][j], at(zl=1 - zl))
        m.send(rows, rows, DIE[g][0][j], at(c=1 - c))

    def j_second(g):
        for j in (0, 3, 1, 2):
            rows = jv.at[g, piece(1 - prim, units[j], c)]
            m.wait(SEC[g][j])
            m.send(rows, rows, DIE[g][1][j], at(c=1 - c))

    def j_finish(g):
        for s in range(2):
            for j in range(4):
                m.wait(DIE[g][s][j])

    R1, R2, R4 = slots(2, 2, 2), slots(2, 2, 4), slots(2, 4)
    put = [pltpu.make_async_copy(nv.at[g, piece(zl, x, c)], out.at[2 * own + g], ls.at[3 + g]) for g in range(2)]

    def n_first(g):
        for kk in range(2):
            for d in range(2):
                k = kk + 2 * d
                m.send(nv.at[g, piece(quad[k][0], xs[2], quad[k][1])], fw.at[g, d, kk], R1[g][d][kk], at(x=xs[1 + 2 * d]))
        for kk in range(2):
            for d in range(2):
                k = kk + 2 - 2 * d
                m.send(nv.at[g, piece(quad[k][0], xs[1 + 2 * d], quad[k][1])], rb.at[g, d, k], R2[g][d][k], at(x=xs[1 + 2 * d]))

    def n_second(g):
        for kk in range(2):
            for d in range(2):
                k = kk + 2 * d
                m.wait(R1[g][d][kk])
                rows = nv.at[g, piece(quad[k][0], xs[1 + 2 * d], quad[k][1])]
                rows[...] += fw[g, d, kk]
                m.send(rows, rb.at[g, d, k], R2[g][d][k], at(x=xs[1 + 2 * d]))

    def n_third(g):
        for k in (2, 3, 1, 0):
            rows = nv.at[g, piece(quad[k][0], x, quad[k][1])]
            m.wait(R2[g][0][k])
            m.wait(R2[g][1][k])
            rows[...] += rb[g, 0, k] + rb[g, 1, k]
            if k == 0:
                put[g].start()
            else:
                m.send(rows, out.at[2 * own + g], R4[g][k], at(zl=quad[k][0], c=quad[k][1]))

    def n_finish(g):
        for k in range(1, 4):
            m.wait(R4[g][k])
        put[g].wait()

    D1, D2, D3, D4, D5 = slots(2, 2, 4), slots(2, 4), slots(2, 4), slots(2, 4), slots(2)
    root_put = pltpu.make_async_copy(fv.at[0, piece(zl, x, c)], extra.at[0], ls.at[5])
    order = (2, 3, 1, 0)

    def f_first(g):
        for s in (1, 0):
            for j in order:
                m.send(fv.at[g, piece(prim if s == 0 else 1 - prim, units[j], 1 - c)], db.at[g, s, j], D1[g][s][j], at(c=1 - c))

    def f_second(g):
        for j in order:
            rows = fv.at[g, piece(1 - prim, units[j], c)]
            m.wait(D1[g][1][j])
            rows[...] += db[g, 1, j]
            m.send(rows, zb.at[g, j], D2[g][j], at(zl=1 - zl))

    def f_third(g):
        for j in order:
            rows = fv.at[g, piece(prim, units[j], c)]
            m.wait(D1[g][0][j])
            m.wait(D2[g][j])
            rows[...] += db[g, 0, j] + zb[g, j]
            m.send(rows, zc.at[g, j], D3[g][j], cross, away[g])

    def f_fourth(g):
        def go():
            for j in order:
                rows = fv.at[g, piece(prim, units[j], c)]
                m.wait(D3[g][j])
                rows[...] += zc[g, j]

        pl.when(home[g])(go)
        via = 3 if g == 0 else 1
        m.send(fv.at[g, piece(prim, units[2], c)], yb.at[g, 2], D4[g][2], at(y=ys[via]), home[g])
        m.send(fv.at[g, piece(prim, units[4 - via], c)], yb.at[g, via], D4[g][via], at(y=ys[4 - via]), home[g])

    def f_fifth(g):
        via = 3 if g == 0 else 1
        rows = fv.at[g, piece(prim, units[via], c)]

        def go():
            m.wait(D4[g][2])
            rows[...] += yb[g, 2]

        pl.when(home[g])(go)
        m.send(rows, yb.at[g, 4 - via], D4[g][4 - via], at(y=ys[via]), home[g])

    def f_sixth(g):
        rows = fv.at[g, piece(prim, units[0], c)]

        def go():
            m.wait(D4[g][1])
            m.wait(D4[g][3])
            rows[...] += yb[g, 1] + yb[g, 3]

        pl.when(home[g])(go)
        if g == 0:
            guarded(at_home_0, root_put.start)
        m.send(rows, extra.at[g], D5[g], source, takes[g])

    def f_finish(g):
        guarded(gives_away[g], lambda: m.wait(D5[g]))
        if g == 0:
            guarded(at_home_0, root_put.wait)

    i_first(0)
    i_spread(0, 0)
    j_first(0)
    i_first(1)
    j_first(1)
    for k in range(1, 4):
        i_spread(0, k)
    j_step(0, 0)
    i_spread(1, 0)
    j_step(0, 3)
    j_step(0, 1)
    i_forward(0)
    j_step(0, 2)
    for k in range(1, 4):
        i_spread(1, k)
    j_second(0)
    for j in (0, 3, 1, 2):
        j_step(1, j)
    i_finish(0)
    j_finish(0)

    def do(*steps):
        def run():
            for step in steps:
                step()

        return run

    plan = {
        (0, 1): do(lambda: i_forward(1), lambda: j_second(1)),
        (1, 0): do(lambda: j_finish(1)),
        (2, 0): do(lambda: n_first(0), lambda: i_finish(1)),
        (2, 2): do(lambda: n_second(0)),
        (3, 0): do(lambda: f_first(1)),
        (3, 1): do(lambda: f_second(1)),
        (3, 2): do(lambda: f_third(1)),
    }

    def point(t, stage):
        for (tt, ss_), run in plan.items():
            if ss_ == stage:
                pl.when(t == tt)(run)

    transform_pairs(iv, jv, nv, fv, a, k_ref, wz_ref, wi_ref, ty_ref, tyi_ref, tx_ref, point)
    n_first(1)
    f_first(0)
    f_fourth(1)
    f_second(0)
    n_second(1)
    n_third(0)
    f_fifth(1)
    f_third(0)
    f_sixth(1)
    n_third(1)
    f_fourth(0)
    f_fifth(0)
    f_sixth(0)
    for g in range(2):
        n_finish(g)
        f_finish(g)
    m.finish()


SENDS, RECEIVES = 256, 256


def run_pairs(own):
    vm = pl.BlockSpec(memory_space=pltpu.VMEM)
    an = pl.BlockSpec(memory_space=pl.ANY)
    f32 = jnp.float32
    big = pltpu.VMEM((2, 6912, 128), f32)

    def pieces(*lead):
        return pltpu.VMEM(lead + (PIECE, 128), f32)

    return pl.pallas_call(
        exchange,
        out_shape=[jax.ShapeDtypeStruct((8, PIECE, 128), f32), jax.ShapeDtypeStruct((2, PIECE, 128), f32)],
        in_specs=[an] + [vm] * 6,
        out_specs=[an, an],
        scratch_shapes=[big] * 4
        + [pltpu.VMEM((96 * 97, 128), f32), pieces(2, 2, 2), pieces(2, 2, 4), pieces(2, 2, 4), pieces(2, 4), pieces(2, 4), pieces(2, 4)]
        + [pltpu.SemaphoreType.DMA((SENDS,)), pltpu.SemaphoreType.DMA((RECEIVES,)), pltpu.SemaphoreType.DMA((8,))],
        compiler_params=pltpu.CompilerParams(vmem_limit_bytes=67043328, collective_id=1, has_side_effects=True),
    )(own, kernel_table(), *tables())


def local(orbitals):
    own = orbitals.reshape(8, PIECE, 128)
    near, far = run_pairs(own)
    gives = lax.axis_index("y") < 2
    out = near.at[0:2].add(jnp.where(gives, far, 0.0))
    return out.reshape(8, 6, 9216)


def solution(mesh):
    fine = jax.sharding.Mesh(mesh.devices.reshape(4, 2, 2, 4, 2), ("y", "zh", "zl", "x", "c"))
    placed = P(("y", "zh"), ("zl", "x", "c"), None)
    return jax.shard_map(local, mesh=fine, in_specs=(placed,), out_specs=placed, check_vma=False)
```

```python
import math, functools
import numpy as np
import jax, jax.numpy as jnp
from jax import lax
from jax.experimental import pallas as pl
from jax.experimental.pallas import tpu as pltpu
from jax.sharding import PartitionSpec as P
import ml_dtypes

N = 96
OMEGA = 0.106
CELL = 41.05
bf = jnp.bfloat16
XB, VB, AS = 24, 24, 97

def split_np(t):
    t = t.astype(np.float32)
    hi = t.astype(ml_dtypes.bfloat16)
    lo = (t - hi.astype(np.float32)).astype(ml_dtypes.bfloat16)
    return hi, lo

def tables():
    k = np.arange(N)
    ang = 2*np.pi*((k[:,None]*k[None,:])%N)/N
    T = np.cos(ang)+np.sin(ang)
    hi, lo = split_np(T)
    wz = np.zeros((4,256,256), ml_dtypes.bfloat16)
    wi = np.zeros((4,256,256), ml_dtypes.bfloat16)
    for l in range(4):
        lane = (96*l + np.arange(N)) % 128
        wz[l, lane, 0:96] = hi
        wz[l, lane, 128:224] = lo
        wz[l, 128+lane, 0:96] = hi
        wi[l, 0:96, lane] = hi.T
        wi[l, 0:96, 128+lane] = lo.T
        wi[l, 128:224, lane] = hi.T
    def two(hi, lo):
        t = np.zeros((192,192), ml_dtypes.bfloat16)
        t[:96,:96]=hi; t[:96,96:]=hi; t[96:,:96]=lo
        return t
    order = np.array([4*kk+l for l in range(4) for kk in range(24)])
    ty = two(hi[:,order], lo[:,order])
    tyi = two(hi[order,:], lo[order,:])
    tx = two(hi, lo)
    return wz, wi, ty, tyi, tx

def kernel_table():
    idx = jnp.arange(N, dtype=jnp.int32)
    f = jnp.where(idx <= N//2, idx, idx-N).astype(jnp.float32)
    sq = f*f
    sqw = jnp.pad(sq, (0,32))
    g2 = (2.0*math.pi/CELL)**2 * (sq[:,None,None]+sq[None,:,None]+sqw[None,None,:])
    pos = g2 > 0
    safe = jnp.where(pos, g2, 1.0)
    val = 4.0*math.pi/safe * -jnp.expm1(-safe/(4.0*OMEGA*OMEGA))
    val = jnp.where(pos, val, math.pi/(OMEGA*OMEGA))
    return (val * (-0.25/float(N**3))).reshape(N*N, 128)

def split(x):
    hi = x.astype(bf)
    lo = (x - hi.astype(jnp.float32)).astype(bf)
    return hi, lo

def dot(a, b):
    return lax.dot_general(a, b, (((1,),(0,)),((),())), preferred_element_type=jnp.float32)

def left(t, x):
    hi, lo = split(x)
    q = dot(t, jnp.concatenate([hi, lo], axis=0))
    return q[:96] + q[96:]

def right(x, w):
    hi, lo = split(x)
    o = dot(jnp.concatenate([hi, lo], axis=1), w)
    return o[:, :128] + o[:, 128:]


def transform_pairs(iv, jv, nv, fv, a_ref, k_ref, wz_ref, wi_ref, ty_ref, tyi_ref, tx_ref, point):
    lane = lax.broadcasted_iota(jnp.int32, (24 * XB, 128), 1)

    def one(t, _):
        gi = t // 2
        gj = ((t + 1) // 2) % 2
        i_ref, j_ref, near_ref, far_ref = iv.at[gi], jv.at[gj], nv.at[gi], fv.at[gj]
        near_first, far_first = gi == gj, gi == 0
        point(t, 0)

        def fwd(xb, _):
            base = xb * (XB * 72)
            d = []
            for s in range(3):
                rows = pl.ds(base + s, 24 * XB, stride=3)
                d.append(i_ref[rows, :] * j_ref[rows, :])
            m = [d[0], jnp.where(lane >= 96, d[0], d[1]), jnp.where(lane >= 64, d[1], d[2]), d[2]]
            o = [right(m[l], wz_ref[l]) for l in range(4)]
            for xx in range(0, XB, 2):
                cols = []
                for x in (xx, xx + 1):
                    cols.append(jnp.concatenate([o[l][24 * x:24 * x + 24] for l in range(4)], axis=0))
                q = left(ty_ref[...], jnp.concatenate(cols, axis=1))
                row = (xb * XB + xx) * AS
                a_ref[pl.ds(row, 96), :] = q[:, :128]
                a_ref[pl.ds(row + AS, 96), :] = q[:, 128:]
            return 0

        lax.fori_loop(0, 96 // XB, fwd, 0)
        point(t, 1)

        def mid(vb, _):
            for vv in range(0, VB, 2):
                v = vb * VB + vv
                b = jnp.concatenate([a_ref[pl.ds(v, 96, stride=AS), :], a_ref[pl.ds(v + 1, 96, stride=AS), :]], axis=1)
                kk = jnp.concatenate([k_ref[pl.ds(v * 96, 96), :], k_ref[pl.ds(v * 96 + 96, 96), :]], axis=1)
                b = left(tx_ref[...], left(tx_ref[...], b) * kk)
                a_ref[pl.ds(v, 96, stride=AS), :] = b[:, :128]
                a_ref[pl.ds(v + 1, 96, stride=AS), :] = b[:, 128:]
            return 0

        lax.fori_loop(0, 96 // VB, mid, 0)
        point(t, 2)

        def inv(xb, _):
            parts = [[] for _ in range(4)]
            for xx in range(0, XB, 2):
                row = (xb * XB + xx) * AS
                b = jnp.concatenate([a_ref[pl.ds(row, 96), :], a_ref[pl.ds(row + AS, 96), :]], axis=1)
                q = left(tyi_ref[...], b)
                for x in range(2):
                    for l in range(4):
                        parts[l].append(q[24 * l:24 * l + 24, 128 * x:128 * x + 128])
            o = [right(jnp.concatenate(parts[l], axis=0), wi_ref[l]) for l in range(4)]
            vs = [jnp.where(lane < 96, o[0], o[1]), jnp.where(lane < 64, o[1], o[2]), jnp.where(lane < 32, o[2], o[3])]
            base = xb * (XB * 72)
            for s in range(3):
                rows = pl.ds(base + s, 24 * XB, stride=3)
                near_ref[rows, :] = jnp.where(near_first, 0.0, near_ref[rows, :]) + j_ref[rows, :] * vs[s]
                far_ref[rows, :] = jnp.where(far_first, 0.0, far_ref[rows, :]) + i_ref[rows, :] * vs[s]
            return 0

        lax.fori_loop(0, 96 // XB, inv, 0)
        return 0

    lax.fori_loop(0, 4, one, 0)


MESH = pl.DeviceIdType.MESH
PIECE = 432


class Comm:
    def __init__(self, ss, rs, some):
        self.ss, self.rs, self.some, self.sent, self.n, self.r = ss, rs, some, [], 0, 0

    def slot(self):
        self.r += 1
        return self.r - 1

    def send(self, src, dst, recv, device, when=None):
        copy = pltpu.make_async_remote_copy(src_ref=src, dst_ref=dst, send_sem=self.ss.at[self.n], recv_sem=self.rs.at[recv],
                                            device_id=device, device_id_type=MESH)
        self.n += 1
        self.sent.append(when)
        guarded(when, copy.start)

    def wait(self, recv):
        pltpu.make_async_copy(self.some, self.some, self.rs.at[recv]).wait()

    def finish(self):
        for n, when in enumerate(self.sent):
            guarded(when, pltpu.make_async_copy(self.some, self.some, self.ss.at[n]).wait)


def guarded(when, do):
    if when is None:
        do()
    else:
        pl.when(when)(lambda: do())


def piece(zl, x, c):
    return pl.ds(pl.multiple_of((zl * 8 + x * 2 + c) * PIECE, PIECE), PIECE)


def exchange(o, k_ref, wz_ref, wi_ref, ty_ref, tyi_ref, tx_ref, out, extra, iv, jv, nv, fv, a, fw, rb, db, zb, yb, ss, rs, ls):
    y, zh, zl, x, c = (lax.axis_index(n) for n in ("y", "zh", "zl", "x", "c"))
    xs = [lax.rem(x + d, 4) for d in range(4)]
    ys = [lax.rem(y + d, 4) for d in range(4)]
    own = 2 * zl + c
    quad = [(zl if k < 2 else 1 - zl, c if k % 2 == 0 else 1 - c) for k in range(4)]
    root_y, root_zh = lax.div(x, 2), lax.rem(x, 2)
    dy = lax.rem(y + 4 - root_y, 4)
    in_root_zh = zh == root_zh
    home = [in_root_zh, jnp.logical_not(in_root_zh)]
    away = [home[1], home[0]]
    prim = jnp.where(in_root_zh, zl, 1 - zl)
    band = 2 * y + zh
    gives = y < 2
    shift = lax.rem(x + 8 - band, 4)
    units = [lax.rem(x + dy + j, 4) for j in range(4)]

    def at(y=y, zh=zh, zl=zl, x=x, c=c):
        return (y, zh, zl, x, c)

    entry = [at(x=lax.rem(band, 4), y=lax.rem(y + shift, 4)), at(x=lax.rem(band, 4), y=lax.rem(y + shift, 4), zh=1 - zh, zl=1 - zl)]
    source = at(x=units[0], y=root_y, zh=root_zh, zl=prim)
    at_home_0 = jnp.logical_and(in_root_zh, dy == 0)
    gives_away = [jnp.logical_and(gives, shift != 0), gives]
    takes = [jnp.logical_and(in_root_zh, dy != 0), home[1]]
    gets = jnp.logical_not(at_home_0)

    barrier = pltpu.get_barrier_semaphore()
    cross = at(zh=1 - zh, zl=1 - zl)
    opposite = at(zh=1 - zh)
    friends = [at(x=xs[d]) for d in range(1, 4)] + [at(y=ys[d]) for d in range(1, 4)] + [cross, opposite]
    friends += [at(zl=qz, c=qc) for qz, qc in quad[1:]]
    for f in friends:
        pl.semaphore_signal(barrier, inc=1, device_id=f, device_id_type=MESH)
    for g in range(2):
        guarded(gives_away[g], lambda: pl.semaphore_signal(barrier, inc=1, device_id=entry[g], device_id_type=MESH))
    guarded(gets, lambda: pl.semaphore_signal(barrier, inc=1, device_id=source, device_id_type=MESH))
    count = gets.astype(jnp.int32) + gives_away[0].astype(jnp.int32) + gives_away[1].astype(jnp.int32)
    pl.semaphore_wait(barrier, len(friends) + count)

    m = Comm(ss, rs, fw.at[0, 0, 0])

    def slots(*shape):
        return [slots(*shape[1:]) for _ in range(shape[0])] if shape else m.slot()

    S1, S2, S3 = slots(2, 4), slots(2, 2, 4), slots(2, 2, 2)
    J1, ZP, ZS, YR, DIE = slots(2), slots(2), slots(2), slots(2, 2, 4), slots(2, 2, 4)
    kind = [prim, 1 - prim]
    keep = [pltpu.make_async_copy(o.at[2 * own + g], iv.at[g, piece(zl, x, c)], ls.at[g]) for g in range(2)]
    root_keep = pltpu.make_async_copy(o.at[0], jv.at[0, piece(zl, x, c)], ls.at[2])

    def i_first(g):
        for k in range(1, 4):
            qz, qc = quad[k]
            m.send(o.at[2 * (2 * qz + qc) + g], iv.at[g, piece(zl, x, c)], S1[g][k], at(zl=qz, c=qc))
        keep[g].start()

    def i_spread(g, k):
        rows = piece(quad[k][0], x, quad[k][1])
        src = iv.at[g, rows]
        if k == 0:
            src = o.at[2 * own + g]
        else:
            m.wait(S1[g][k])
        for d in range(2):
            m.send(src, iv.at[g, rows], S2[g][d][k], at(x=xs[1 + 2 * d]))

    def i_forward(g):
        for kk in range(2):
            for d in range(2):
                k = kk + 2 * d
                rows = iv.at[g, piece(quad[k][0], xs[3 - 2 * d], quad[k][1])]
                m.wait(S2[g][d][k])
                m.send(rows, rows, S3[g][d][kk], at(x=xs[1 + 2 * d]))

    def i_finish(g):
        keep[g].wait()
        for d in range(2):
            for kk in range(2):
                m.wait(S2[g][d][kk + 2 - 2 * d])
                m.wait(S3[g][d][kk])

    def j_first(g):
        m.send(o.at[g], jv.at[g, piece(zl, x, c)], J1[g], entry[g], gives_away[g])
        if g == 0:
            guarded(at_home_0, root_keep.start)

    def j_row(g, kd):
        rows = jv.at[g, piece(kind[kd], units[0], c)]
        for j in (1, 3, 2):
            m.send(rows, rows, YR[g][kd][4 - j], at(y=ys[j]))
        m.send(rows, rows, DIE[g][kd][0], at(c=1 - c))

    def j_entry(g):
        rows = jv.at[g, piece(prim, units[0], c)]
        if g == 0:
            guarded(at_home_0, root_keep.wait)
        guarded(takes[g], lambda: m.wait(J1[g]))
        m.send(rows, rows, ZP[g], cross, home[g])
        m.send(rows, rows, ZS[g], at(zl=1 - zl), home[g])
        m.send(rows, rows, ZS[g], opposite, home[g])
        guarded(away[g], lambda: m.wait(ZP[g]))
        j_row(g, 0)

    def j_other(g):
        m.wait(ZS[g])
        j_row(g, 1)

    def j_rows(g):
        for kd in range(2):
            for j in (3, 1, 2):
                rows = jv.at[g, piece(kind[kd], units[j], c)]
                m.wait(YR[g][kd][j])
                m.send(rows, rows, DIE[g][kd][j], at(c=1 - c))

    def j_finish(g):
        for s in range(2):
            for j in range(4):
                m.wait(DIE[g][s][j])

    R1, R2, R4 = slots(2, 2, 2), slots(2, 2, 4), slots(2, 4)
    put = [pltpu.make_async_copy(nv.at[g, piece(zl, x, c)], out.at[2 * own + g], ls.at[3 + g]) for g in range(2)]

    def n_first(g):
        for kk in range(2):
            for d in range(2):
                k = kk + 2 * d
                m.send(nv.at[g, piece(quad[k][0], xs[2], quad[k][1])], fw.at[g, d, kk], R1[g][d][kk], at(x=xs[1 + 2 * d]))
        for kk in range(2):
            for d in range(2):
                k = kk + 2 - 2 * d
                m.send(nv.at[g, piece(quad[k][0], xs[1 + 2 * d], quad[k][1])], rb.at[g, d, k], R2[g][d][k], at(x=xs[1 + 2 * d]))

    def n_second(g):
        for kk in range(2):
            for d in range(2):
                k = kk + 2 * d
                m.wait(R1[g][d][kk])
                rows = nv.at[g, piece(quad[k][0], xs[1 + 2 * d], quad[k][1])]
                rows[...] += fw[g, d, kk]
                m.send(rows, rb.at[g, d, k], R2[g][d][k], at(x=xs[1 + 2 * d]))

    def n_third(g):
        for k in (2, 3, 1, 0):
            rows = nv.at[g, piece(quad[k][0], x, quad[k][1])]
            m.wait(R2[g][0][k])
            m.wait(R2[g][1][k])
            rows[...] += rb[g, 0, k] + rb[g, 1, k]
            if k == 0:
                put[g].start()
            else:
                m.send(rows, out.at[2 * own + g], R4[g][k], at(zl=quad[k][0], c=quad[k][1]))

    def n_finish(g):
        for k in range(1, 4):
            m.wait(R4[g][k])
        put[g].wait()

    D1, D2, D3, D5 = slots(2, 2, 4), slots(2, 2, 4), slots(2, 3), slots(2)
    root_put = pltpu.make_async_copy(fv.at[0, piece(zl, x, c)], extra.at[0], ls.at[5])

    def f_first(g):
        for j in (2, 1, 3, 0):
            for kd in range(2):
                m.send(fv.at[g, piece(kind[kd], units[j], 1 - c)], db.at[g, kd, j], D1[g][kd][j], at(c=1 - c))

    def f_second(g):
        for j in (2, 1, 3, 0):
            for kd in (1, 0):
                rows = fv.at[g, piece(kind[kd], units[j], c)]
                m.wait(D1[g][kd][j])
                rows[...] += db[g, kd, j]
                if j:
                    m.send(rows, yb.at[g, kd, j], D2[g][kd][j], at(y=ys[j]))

    def f_third(g):
        for kd in (1, 0):
            rows = fv.at[g, piece(kind[kd], units[0], c)]
            for j in (1, 3, 2):
                m.wait(D2[g][kd][j])
            rows[...] += (yb[g, kd, 1] + yb[g, kd, 2]) + yb[g, kd, 3]
            if kd:
                m.send(rows, zb.at[g, 0], D3[g][0], at(zl=1 - zl), home[g])
                m.send(rows, zb.at[g, 1], D3[g][1], opposite, away[g])
            else:
                m.send(rows, zb.at[g, 2], D3[g][2], cross, away[g])

    def f_fourth(g):
        rows = fv.at[g, piece(prim, units[0], c)]

        def go():
            for e in range(3):
                m.wait(D3[g][e])
            rows[...] += (zb[g, 0] + zb[g, 1]) + zb[g, 2]

        pl.when(home[g])(go)
        if g == 0:
            guarded(at_home_0, root_put.start)
        m.send(rows, extra.at[g], D5[g], source, takes[g])

    def f_finish(g):
        guarded(gives_away[g], lambda: m.wait(D5[g]))
        if g == 0:
            guarded(at_home_0, root_put.wait)

    i_first(0)
    i_spread(0, 0)
    j_first(0)
    i_first(1)
    j_first(1)
    for k in range(1, 4):
        i_spread(0, k)
    j_entry(0)
    i_spread(1, 0)
    j_entry(1)
    j_other(0)
    i_forward(0)
    j_other(1)
    for k in range(1, 4):
        i_spread(1, k)
    j_rows(0)
    i_finish(0)
    j_finish(0)

    def do(*steps):
        def run():
            for step in steps:
                step()

        return run

    plan = {
        (0, 1): do(lambda: j_rows(1)),
        (0, 2): do(lambda: i_forward(1)),
        (1, 0): do(lambda: j_finish(1)),
        (2, 0): do(lambda: n_first(0), lambda: i_finish(1)),
        (2, 2): do(lambda: n_second(0)),
        (3, 0): do(lambda: f_first(1)),
        (3, 1): do(lambda: f_second(1)),
        (3, 2): do(lambda: n_third(0)),
    }

    def point(t, stage):
        for (tt, ss_), run in plan.items():
            if ss_ == stage:
                pl.when(t == tt)(run)

    transform_pairs(iv, jv, nv, fv, a, k_ref, wz_ref, wi_ref, ty_ref, tyi_ref, tx_ref, point)
    n_first(1)
    f_first(0)
    f_second(0)
    f_third(1)
    n_second(1)
    f_fourth(1)
    f_third(0)
    f_fourth(0)
    n_third(1)
    for g in range(2):
        n_finish(g)
        f_finish(g)
    m.finish()


SENDS, RECEIVES = 256, 256


def run_pairs(own):
    vm = pl.BlockSpec(memory_space=pltpu.VMEM)
    an = pl.BlockSpec(memory_space=pl.ANY)
    f32 = jnp.float32
    big = pltpu.VMEM((2, 6912, 128), f32)

    def pieces(*lead):
        return pltpu.VMEM(lead + (PIECE, 128), f32)

    return pl.pallas_call(
        exchange,
        out_shape=[jax.ShapeDtypeStruct((8, PIECE, 128), f32), jax.ShapeDtypeStruct((2, PIECE, 128), f32)],
        in_specs=[an] + [vm] * 6,
        out_specs=[an, an],
        scratch_shapes=[big] * 4
        + [pltpu.VMEM((96 * 97, 128), f32), pieces(2, 2, 2), pieces(2, 2, 4), pieces(2, 2, 4), pieces(2, 3), pieces(2, 2, 4)]
        + [pltpu.SemaphoreType.DMA((SENDS,)), pltpu.SemaphoreType.DMA((RECEIVES,)), pltpu.SemaphoreType.DMA((8,))],
        compiler_params=pltpu.CompilerParams(vmem_limit_bytes=67043328, collective_id=1, has_side_effects=True),
    )(own, kernel_table(), *tables())


def local(orbitals):
    own = orbitals.reshape(8, PIECE, 128)
    near, far = run_pairs(own)
    gives = lax.axis_index("y") < 2
    out = near.at[0:2].add(jnp.where(gives, far, 0.0))
    return out.reshape(8, 6, 9216)


def solution(mesh):
    fine = jax.sharding.Mesh(mesh.devices.reshape(4, 2, 2, 4, 2), ("y", "zh", "zl", "x", "c"))
    placed = P(("y", "zh"), ("zl", "x", "c"), None)
    return jax.shard_map(local, mesh=fine, in_specs=(placed,), out_specs=placed, check_vma=False)
```

```python
import math, functools
import numpy as np
import jax, jax.numpy as jnp
from jax import lax
from jax.experimental import pallas as pl
from jax.experimental.pallas import tpu as pltpu
from jax.sharding import PartitionSpec as P
import ml_dtypes

N = 96
OMEGA = 0.106
CELL = 41.05
bf = jnp.bfloat16
XB, VB, AS = 24, 24, 97

def split_np(t):
    t = t.astype(np.float32)
    hi = t.astype(ml_dtypes.bfloat16)
    lo = (t - hi.astype(np.float32)).astype(ml_dtypes.bfloat16)
    return hi, lo

def tables():
    k = np.arange(N)
    ang = 2*np.pi*((k[:,None]*k[None,:])%N)/N
    T = np.cos(ang)+np.sin(ang)
    hi, lo = split_np(T)
    wz = np.zeros((4,256,256), ml_dtypes.bfloat16)
    wi = np.zeros((4,256,256), ml_dtypes.bfloat16)
    for l in range(4):
        lane = (96*l + np.arange(N)) % 128
        wz[l, lane, 0:96] = hi
        wz[l, lane, 128:224] = lo
        wz[l, 128+lane, 0:96] = hi
        wi[l, 0:96, lane] = hi.T
        wi[l, 0:96, 128+lane] = lo.T
        wi[l, 128:224, lane] = hi.T
    def two(hi, lo):
        t = np.zeros((192,192), ml_dtypes.bfloat16)
        t[:96,:96]=hi; t[:96,96:]=hi; t[96:,:96]=lo
        return t
    order = np.array([4*kk+l for l in range(4) for kk in range(24)])
    ty = two(hi[:,order], lo[:,order])
    tyi = two(hi[order,:], lo[order,:])
    tx = two(hi, lo)
    return wz, wi, ty, tyi, tx

def build_kernel(k_ref):
    def square(index):
        index = index.astype(jnp.float32)
        freq = jnp.where(index <= N // 2, index, index - N)
        return freq * freq

    u = square(lax.broadcasted_iota(jnp.int32, (N, 128), 0))
    w = square(jnp.minimum(lax.broadcasted_iota(jnp.int32, (N, 128), 1), N - 1))
    plane = u + w
    scale = (2.0 * math.pi / CELL) ** 2
    factor = -0.25 / float(N**3)

    def one(v, _):
        g_two = scale * (plane + square(v))
        positive = g_two > 0
        safe = jnp.where(positive, g_two, 1.0)
        value = (4.0 * math.pi * factor) / safe * (1.0 - jnp.exp(safe * (-1.0 / (4.0 * OMEGA * OMEGA))))
        k_ref[pl.ds(pl.multiple_of(v * N, 8), N), :] = jnp.where(positive, value, math.pi / (OMEGA * OMEGA) * factor)
        return 0

    lax.fori_loop(0, N, one, 0)


def split(x):
    hi = x.astype(bf)
    lo = (x - hi.astype(jnp.float32)).astype(bf)
    return hi, lo

def dot(a, b):
    return lax.dot_general(a, b, (((1,),(0,)),((),())), preferred_element_type=jnp.float32)

def left(t, x):
    hi, lo = split(x)
    q = dot(t, jnp.concatenate([hi, lo], axis=0))
    return q[:96] + q[96:]

def right(x, w):
    hi, lo = split(x)
    o = dot(jnp.concatenate([hi, lo], axis=1), w)
    return o[:, :128] + o[:, 128:]


def transform_pairs(iv, jv, nv, fv, a_ref, k_ref, wz_ref, wi_ref, ty_ref, tyi_ref, tx_ref, point):
    lane = lax.broadcasted_iota(jnp.int32, (24 * XB, 128), 1)

    def one(t, _):
        gi = t // 2
        gj = ((t + 1) // 2) % 2
        i_ref, j_ref, near_ref, far_ref = iv.at[gi], jv.at[gj], nv.at[gi], fv.at[gj]
        near_first, far_first = gi == gj, gi == 0
        point(t, 0)

        def fwd(xb, _):
            base = xb * (XB * 72)
            d = []
            for s in range(3):
                rows = pl.ds(base + s, 24 * XB, stride=3)
                d.append(i_ref[rows, :] * j_ref[rows, :])
            m = [d[0], jnp.where(lane >= 96, d[0], d[1]), jnp.where(lane >= 64, d[1], d[2]), d[2]]
            o = [right(m[l], wz_ref[l]) for l in range(4)]
            for xx in range(0, XB, 2):
                cols = []
                for x in (xx, xx + 1):
                    cols.append(jnp.concatenate([o[l][24 * x:24 * x + 24] for l in range(4)], axis=0))
                q = left(ty_ref[...], jnp.concatenate(cols, axis=1))
                row = (xb * XB + xx) * AS
                a_ref[pl.ds(row, 96), :] = q[:, :128]
                a_ref[pl.ds(row + AS, 96), :] = q[:, 128:]
            return 0

        lax.fori_loop(0, 96 // XB, fwd, 0)
        point(t, 1)

        def mid(vb, _):
            for vv in range(0, VB, 2):
                v = vb * VB + vv
                b = jnp.concatenate([a_ref[pl.ds(v, 96, stride=AS), :], a_ref[pl.ds(v + 1, 96, stride=AS), :]], axis=1)
                kk = jnp.concatenate([k_ref[pl.ds(v * 96, 96), :], k_ref[pl.ds(v * 96 + 96, 96), :]], axis=1)
                b = left(tx_ref[...], left(tx_ref[...], b) * kk)
                a_ref[pl.ds(v, 96, stride=AS), :] = b[:, :128]
                a_ref[pl.ds(v + 1, 96, stride=AS), :] = b[:, 128:]
            return 0

        lax.fori_loop(0, 96 // VB, mid, 0)
        point(t, 2)

        def inv(xb, _):
            parts = [[] for _ in range(4)]
            for xx in range(0, XB, 2):
                row = (xb * XB + xx) * AS
                b = jnp.concatenate([a_ref[pl.ds(row, 96), :], a_ref[pl.ds(row + AS, 96), :]], axis=1)
                q = left(tyi_ref[...], b)
                for x in range(2):
                    for l in range(4):
                        parts[l].append(q[24 * l:24 * l + 24, 128 * x:128 * x + 128])
            o = [right(jnp.concatenate(parts[l], axis=0), wi_ref[l]) for l in range(4)]
            vs = [jnp.where(lane < 96, o[0], o[1]), jnp.where(lane < 64, o[1], o[2]), jnp.where(lane < 32, o[2], o[3])]
            base = xb * (XB * 72)
            for s in range(3):
                rows = pl.ds(base + s, 24 * XB, stride=3)
                near_ref[rows, :] = jnp.where(near_first, 0.0, near_ref[rows, :]) + j_ref[rows, :] * vs[s]
                far_ref[rows, :] = jnp.where(far_first, 0.0, far_ref[rows, :]) + i_ref[rows, :] * vs[s]
            return 0

        lax.fori_loop(0, 96 // XB, inv, 0)
        return 0

    lax.fori_loop(0, 4, one, 0)


MESH = pl.DeviceIdType.MESH
PIECE = 432


class Comm:
    def __init__(self, ss, rs, some):
        self.ss, self.rs, self.some, self.sent, self.n, self.r = ss, rs, some, [], 0, 0

    def slot(self):
        self.r += 1
        return self.r - 1

    def send(self, src, dst, recv, device, when=None):
        copy = pltpu.make_async_remote_copy(src_ref=src, dst_ref=dst, send_sem=self.ss.at[self.n], recv_sem=self.rs.at[recv],
                                            device_id=device, device_id_type=MESH)
        self.n += 1
        self.sent.append(when)
        guarded(when, copy.start)

    def wait(self, recv):
        pltpu.make_async_copy(self.some, self.some, self.rs.at[recv]).wait()

    def finish(self):
        for n, when in enumerate(self.sent):
            guarded(when, pltpu.make_async_copy(self.some, self.some, self.ss.at[n]).wait)


def guarded(when, do):
    if when is None:
        do()
    else:
        pl.when(when)(lambda: do())


def piece(zl, x, c):
    return pl.ds(pl.multiple_of((zl * 8 + x * 2 + c) * PIECE, PIECE), PIECE)


def exchange(orbitals, wz_ref, wi_ref, ty_ref, tyi_ref, tx_ref, action, k_ref, planes, o, out, extra, hb, iv, jv, nv, fv, a, fw, rb, db, zb, yb, ss, rs, ls):
    fetch = [pltpu.make_async_copy(orbitals.at[b], planes.at[b], ls.at[8 + b]) for b in range(6)]
    for copy in fetch:
        copy.start()
    y, zh, zl, x, c = (lax.axis_index(n) for n in ("y", "zh", "zl", "x", "c"))
    xs = [lax.rem(x + d, 4) for d in range(4)]
    ys = [lax.rem(y + d, 4) for d in range(4)]
    own = 2 * zl + c
    quad = [(zl if k < 2 else 1 - zl, c if k % 2 == 0 else 1 - c) for k in range(4)]
    root_y, root_zh = lax.div(x, 2), lax.rem(x, 2)
    dy = lax.rem(y + 4 - root_y, 4)
    in_root_zh = zh == root_zh
    home = [in_root_zh, jnp.logical_not(in_root_zh)]
    away = [home[1], home[0]]
    prim = jnp.where(in_root_zh, zl, 1 - zl)
    band = 2 * y + zh
    gives = y < 2
    shift = lax.rem(x + 8 - band, 4)
    units = [lax.rem(x + dy + j, 4) for j in range(4)]

    def at(y=y, zh=zh, zl=zl, x=x, c=c):
        return (y, zh, zl, x, c)

    relay = [at(y=lax.rem(y + shift, 4)), at(y=lax.rem(y + shift, 4), zh=1 - zh, zl=1 - zl)]
    source = at(x=units[0], y=root_y, zh=root_zh, zl=prim)
    at_home_0 = jnp.logical_and(in_root_zh, dy == 0)
    gives_away = [jnp.logical_and(gives, shift != 0), gives]
    diagonal = lax.rem(x + 4 - y, 4)
    is_relay, passes, passed_to, passed_from = [], [], [], []
    for g in range(2):
        zr = zh if g == 0 else 1 - zh
        second = jnp.where(diagonal == zr, 0, 1)
        target = zr + 2 * second
        on_path = jnp.logical_or(diagonal == zr, diagonal == zr + 1)
        moves = jnp.logical_and(on_path, x != target)
        is_relay.append(moves if g == 0 else on_path)
        passes.append(moves)
        passed_to.append(at(x=target))
        passed_from.append(at(y=second, zh=zr, zl=zl if g == 0 else 1 - zl))
    stays = jnp.logical_and(is_relay[1], jnp.logical_not(passes[1]))
    takes = [jnp.logical_and(in_root_zh, dy != 0), home[1]]
    arrives = [takes[0], jnp.logical_and(takes[1], dy != 0)]

    barrier = pltpu.get_barrier_semaphore()
    cross = at(zh=1 - zh, zl=1 - zl)
    opposite = at(zh=1 - zh)
    friends = [at(x=xs[d]) for d in range(1, 4)] + [at(y=ys[d]) for d in range(1, 4)] + [cross, opposite]
    friends += [at(zl=qz, c=qc) for qz, qc in quad[1:]]
    for f in friends:
        pl.semaphore_signal(barrier, inc=1, device_id=f, device_id_type=MESH)
    for g in range(2):
        guarded(gives_away[g], lambda: pl.semaphore_signal(barrier, inc=1, device_id=relay[g], device_id_type=MESH))
        guarded(is_relay[g], lambda: pl.semaphore_signal(barrier, inc=1, device_id=passed_from[g], device_id_type=MESH))
    count = sum(flag.astype(jnp.int32) for flag in gives_away + is_relay)
    for copy in fetch:
        copy.wait()

    def unpack(b, _):
        for q in range(72):
            o[pl.ds(b * 72 + q, 8, stride=PIECE), :] = planes[b, :, 128 * q:128 * q + 128]
        return 0

    lax.fori_loop(0, 6, unpack, 0)
    pl.semaphore_wait(barrier, len(friends) + count)

    m = Comm(ss, rs, fw.at[0, 0, 0])

    def orbital(ref, b):
        return ref.at[pl.ds(pl.multiple_of(b * PIECE, PIECE), PIECE)]


    def slots(*shape):
        return [slots(*shape[1:]) for _ in range(shape[0])] if shape else m.slot()

    S1, S2, S3 = slots(2, 4), slots(2, 2, 4), slots(2, 2, 2)
    JA, J1, ZP, ZS, YR, DIE = slots(2), slots(2), slots(2), slots(2), slots(2, 2, 4), slots(2, 2, 4)
    kind = [prim, 1 - prim]
    keep = [pltpu.make_async_copy(orbital(o, 2 * own + g), iv.at[g, piece(zl, x, c)], ls.at[g]) for g in range(2)]
    root_keep = pltpu.make_async_copy(orbital(o, 0), jv.at[0, piece(zl, x, c)], ls.at[2])

    def i_first(g):
        for k in range(1, 4):
            qz, qc = quad[k]
            m.send(orbital(o, 2 * (2 * qz + qc) + g), iv.at[g, piece(zl, x, c)], S1[g][k], at(zl=qz, c=qc))
        keep[g].start()

    def i_spread(g, k):
        rows = piece(quad[k][0], x, quad[k][1])
        src = iv.at[g, rows]
        if k == 0:
            src = orbital(o, 2 * own + g)
        else:
            m.wait(S1[g][k])
        for d in range(2):
            m.send(src, iv.at[g, rows], S2[g][d][k], at(x=xs[1 + 2 * d]))

    def i_forward(g):
        for kk in range(2):
            for d in range(2):
                k = kk + 2 * d
                rows = iv.at[g, piece(quad[k][0], xs[3 - 2 * d], quad[k][1])]
                m.wait(S2[g][d][k])
                m.send(rows, rows, S3[g][d][kk], at(x=xs[1 + 2 * d]))

    def i_finish(g):
        keep[g].wait()
        for d in range(2):
            for kk in range(2):
                m.wait(S2[g][d][kk + 2 - 2 * d])
                m.wait(S3[g][d][kk])

    stay = pltpu.make_async_copy(hb.at[0, 1], jv.at[1, piece(prim, units[0], c)], ls.at[6])

    def j_first(g):
        m.send(orbital(o, g), hb.at[0, g], JA[g], relay[g], gives_away[g])
        if g == 0:
            guarded(at_home_0, root_keep.start)

    def j_relay(g):
        guarded(is_relay[g], lambda: m.wait(JA[g]))
        m.send(hb.at[0, g], jv.at[g, piece(zl if g == 0 else 1 - zl, x, c)], J1[g], passed_to[g], passes[g])
        if g == 1:
            guarded(stays, stay.start)

    def j_row(g, kd):
        rows = jv.at[g, piece(kind[kd], units[0], c)]
        for j in (1, 3, 2):
            m.send(rows, rows, YR[g][kd][4 - j], at(y=ys[j]))
        m.send(rows, rows, DIE[g][kd][0], at(c=1 - c))

    def j_entry(g):
        rows = jv.at[g, piece(prim, units[0], c)]
        if g == 0:
            guarded(at_home_0, root_keep.wait)
        else:
            guarded(stays, stay.wait)
        guarded(arrives[g], lambda: m.wait(J1[g]))
        m.send(rows, rows, ZP[g], cross, home[g])
        m.send(rows, rows, ZS[g], at(zl=1 - zl), home[g])
        m.send(rows, rows, ZS[g], opposite, home[g])
        guarded(away[g], lambda: m.wait(ZP[g]))
        j_row(g, 0)

    def j_other(g):
        m.wait(ZS[g])
        j_row(g, 1)

    def j_rows(g):
        for kd in range(2):
            for j in (3, 1, 2):
                rows = jv.at[g, piece(kind[kd], units[j], c)]
                m.wait(YR[g][kd][j])
                m.send(rows, rows, DIE[g][kd][j], at(c=1 - c))

    def j_finish(g):
        for s in range(2):
            for j in range(4):
                m.wait(DIE[g][s][j])

    R1, R2, R4 = slots(2, 2, 2), slots(2, 2, 4), slots(2, 4)
    put = [pltpu.make_async_copy(nv.at[g, piece(zl, x, c)], orbital(out, 2 * own + g), ls.at[3 + g]) for g in range(2)]

    def n_first(g):
        for kk in range(2):
            for d in range(2):
                k = kk + 2 * d
                m.send(nv.at[g, piece(quad[k][0], xs[2], quad[k][1])], fw.at[g, d, kk], R1[g][d][kk], at(x=xs[1 + 2 * d]))
        for kk in range(2):
            for d in range(2):
                k = kk + 2 - 2 * d
                m.send(nv.at[g, piece(quad[k][0], xs[1 + 2 * d], quad[k][1])], rb.at[g, d, k], R2[g][d][k], at(x=xs[1 + 2 * d]))

    def n_second(g):
        for kk in range(2):
            for d in range(2):
                k = kk + 2 * d
                m.wait(R1[g][d][kk])
                rows = nv.at[g, piece(quad[k][0], xs[1 + 2 * d], quad[k][1])]
                rows[...] += fw[g, d, kk]
                m.send(rows, rb.at[g, d, k], R2[g][d][k], at(x=xs[1 + 2 * d]))

    def n_third(g):
        for k in (2, 3, 1, 0):
            rows = nv.at[g, piece(quad[k][0], x, quad[k][1])]
            m.wait(R2[g][0][k])
            m.wait(R2[g][1][k])
            rows[...] += rb[g, 0, k] + rb[g, 1, k]
            if k == 0:
                put[g].start()
            else:
                m.send(rows, orbital(out, 2 * own + g), R4[g][k], at(zl=quad[k][0], c=quad[k][1]))

    def n_finish(g):
        for k in range(1, 4):
            m.wait(R4[g][k])
        put[g].wait()

    D1, D2, D3, D5, D6 = slots(2, 2, 4), slots(2, 2, 4), slots(2, 3), slots(2), slots(2)
    root_put = pltpu.make_async_copy(fv.at[0, piece(zl, x, c)], extra.at[0], ls.at[5])

    def f_first(g):
        for j in (2, 1, 3, 0):
            for kd in range(2):
                m.send(fv.at[g, piece(kind[kd], units[j], 1 - c)], db.at[g, kd, j], D1[g][kd][j], at(c=1 - c))

    def f_second(g):
        for j in (2, 1, 3, 0):
            for kd in (1, 0):
                rows = fv.at[g, piece(kind[kd], units[j], c)]
                m.wait(D1[g][kd][j])
                rows[...] += db[g, kd, j]
                if j:
                    m.send(rows, yb.at[g, kd, j], D2[g][kd][j], at(y=ys[j]))

    def f_third(g):
        for kd in (1, 0):
            rows = fv.at[g, piece(kind[kd], units[0], c)]
            for j in (1, 3, 2):
                m.wait(D2[g][kd][j])
            rows[...] += (yb[g, kd, 1] + yb[g, kd, 2]) + yb[g, kd, 3]
            if kd:
                m.send(rows, zb.at[g, 0], D3[g][0], at(zl=1 - zl), home[g])
                m.send(rows, zb.at[g, 1], D3[g][1], opposite, away[g])
            else:
                m.send(rows, zb.at[g, 2], D3[g][2], cross, away[g])

    def f_fourth(g):
        rows = fv.at[g, piece(prim, units[0], c)]

        def go():
            for e in range(3):
                m.wait(D3[g][e])
            rows[...] += (zb[g, 0] + zb[g, 1]) + zb[g, 2]

        pl.when(home[g])(go)
        if g == 0:
            guarded(at_home_0, root_put.start)
        m.send(rows, hb.at[1, g], D5[g], at(x=units[0]), arrives[g])
        if g == 1:
            m.send(rows, extra.at[g], D6[g], source, stays)

    def f_fifth(g):
        guarded(passes[g], lambda: m.wait(D5[g]))
        m.send(hb.at[1, g], extra.at[g], D6[g], passed_from[g], passes[g])

    def f_finish(g):
        guarded(gives_away[g], lambda: m.wait(D6[g]))
        if g == 0:
            guarded(at_home_0, root_put.wait)

    j_first(0)
    i_first(0)
    i_spread(0, 0)
    j_first(1)
    i_first(1)
    build_kernel(k_ref)
    for k in range(1, 4):
        i_spread(0, k)
    j_relay(0)
    j_relay(1)
    j_entry(0)
    i_spread(1, 0)
    j_entry(1)
    j_other(0)
    i_forward(0)
    j_other(1)
    for k in range(1, 4):
        i_spread(1, k)
    j_rows(0)
    i_finish(0)
    j_finish(0)

    def do(*steps):
        def run():
            for step in steps:
                step()

        return run

    plan = {
        (0, 1): do(lambda: j_rows(1)),
        (0, 2): do(lambda: i_forward(1)),
        (1, 0): do(lambda: j_finish(1)),
        (2, 0): do(lambda: n_first(0), lambda: i_finish(1)),
        (2, 2): do(lambda: n_second(0)),
        (3, 0): do(lambda: f_first(1)),
        (3, 1): do(lambda: f_second(1)),
        (3, 2): do(lambda: n_third(0)),
    }

    def point(t, stage):
        for (tt, ss_), run in plan.items():
            if ss_ == stage:
                pl.when(t == tt)(run)

    transform_pairs(iv, jv, nv, fv, a, k_ref, wz_ref, wi_ref, ty_ref, tyi_ref, tx_ref, point)
    n_first(1)
    f_first(0)
    f_second(0)
    f_third(1)
    n_second(1)
    f_fourth(1)
    f_third(0)
    f_fifth(1)
    f_fourth(0)
    n_third(1)
    f_fifth(0)
    for g in range(2):
        n_finish(g)
        f_finish(g)

    for g in range(2):

        def add():
            out[pl.ds(g * PIECE, PIECE), :] += extra[g]

        pl.when(gives)(add)

    def pack(b, _):
        for q in range(72):
            planes[b, :, 128 * q:128 * q + 128] = out[pl.ds(b * 72 + q, 8, stride=PIECE), :]
        return 0

    lax.fori_loop(0, 6, pack, 0)
    stores = [pltpu.make_async_copy(planes.at[b], action.at[b], ls.at[8 + b]) for b in range(6)]
    for store in stores:
        store.start()
    m.finish()
    for store in stores:
        store.wait()


SENDS, RECEIVES = 256, 256


def local(orbitals):
    vm = pl.BlockSpec(memory_space=pltpu.VMEM)
    an = pl.BlockSpec(memory_space=pl.ANY)
    f32 = jnp.float32
    big = pltpu.VMEM((2, 6912, 128), f32)

    def pieces(*lead):
        return pltpu.VMEM(lead + (PIECE, 128), f32)

    return pl.pallas_call(
        exchange,
        out_shape=jax.ShapeDtypeStruct((6, 8, 9216), f32),
        in_specs=[an] + [vm] * 5,
        out_specs=an,
        scratch_shapes=[pltpu.VMEM((N * N, 128), f32), pltpu.VMEM((6, 8, 9216), f32), pltpu.VMEM((8 * PIECE, 128), f32), pltpu.VMEM((8 * PIECE, 128), f32), pieces(2), pieces(2, 2)]
        + [big] * 4
        + [pltpu.VMEM((96 * AS, 128), f32), pieces(2, 2, 2), pieces(2, 2, 4), pieces(2, 2, 4), pieces(2, 3), pieces(2, 2, 4)]
        + [pltpu.SemaphoreType.DMA((SENDS,)), pltpu.SemaphoreType.DMA((RECEIVES,)), pltpu.SemaphoreType.DMA((16,))],
        compiler_params=pltpu.CompilerParams(vmem_limit_bytes=67043328, collective_id=1, has_side_effects=True),
    )(orbitals.transpose(1, 0, 2), *tables()).transpose(1, 0, 2)


def solution(mesh):
    fine = jax.sharding.Mesh(mesh.devices.reshape(4, 2, 2, 4, 2), ("y", "zh", "zl", "x", "c"))
    placed = P(("y", "zh"), ("zl", "x", "c"), None)
    return jax.shard_map(local, mesh=fine, in_specs=(placed,), out_specs=placed, check_vma=False)
```

```python
import math, functools
import numpy as np
import jax, jax.numpy as jnp
from jax import lax
from jax.experimental import pallas as pl
from jax.experimental.pallas import tpu as pltpu
from jax.sharding import PartitionSpec as P
import ml_dtypes

N = 96
OMEGA = 0.106
CELL = 41.05
bf = jnp.bfloat16
XB, VB, AS = 24, 24, 97

def split_np(t):
    t = t.astype(np.float32)
    hi = t.astype(ml_dtypes.bfloat16)
    lo = (t - hi.astype(np.float32)).astype(ml_dtypes.bfloat16)
    return hi, lo

def tables():
    k = np.arange(N)
    ang = 2*np.pi*((k[:,None]*k[None,:])%N)/N
    T = np.cos(ang)+np.sin(ang)
    hi, lo = split_np(T)
    wz = np.zeros((4,256,256), ml_dtypes.bfloat16)
    wi = np.zeros((4,256,256), ml_dtypes.bfloat16)
    for l in range(4):
        lane = (96*l + np.arange(N)) % 128
        wz[l, lane, 0:96] = hi
        wz[l, lane, 128:224] = lo
        wz[l, 128+lane, 0:96] = hi
        wi[l, 0:96, lane] = hi.T
        wi[l, 0:96, 128+lane] = lo.T
        wi[l, 128:224, lane] = hi.T
    def two(hi, lo):
        t = np.zeros((192,192), ml_dtypes.bfloat16)
        t[:96,:96]=hi; t[:96,96:]=hi; t[96:,:96]=lo
        return t
    order = np.array([4*kk+l for l in range(4) for kk in range(24)])
    ty = two(hi[:,order], lo[:,order])
    tyi = two(hi[order,:], lo[order,:])
    tx = two(hi, lo)
    return wz, wi, ty, tyi, tx

def build_kernel(k_ref):
    def square(index):
        index = index.astype(jnp.float32)
        freq = jnp.where(index <= N // 2, index, index - N)
        return freq * freq

    u = square(lax.broadcasted_iota(jnp.int32, (N, 128), 0))
    w = square(jnp.minimum(lax.broadcasted_iota(jnp.int32, (N, 128), 1), N - 1))
    plane = u + w
    scale = (2.0 * math.pi / CELL) ** 2
    factor = -0.25 / float(N**3)

    def one(v, _):
        g_two = scale * (plane + square(v))
        positive = g_two > 0
        safe = jnp.where(positive, g_two, 1.0)
        value = (4.0 * math.pi * factor) / safe * (1.0 - jnp.exp(safe * (-1.0 / (4.0 * OMEGA * OMEGA))))
        k_ref[pl.ds(pl.multiple_of(v * N, 8), N), :] = jnp.where(positive, value, math.pi / (OMEGA * OMEGA) * factor)
        return 0

    lax.fori_loop(0, N, one, 0)


def split(x):
    hi = x.astype(bf)
    lo = (x - hi.astype(jnp.float32)).astype(bf)
    return hi, lo

def dot(a, b):
    return lax.dot_general(a, b, (((1,),(0,)),((),())), preferred_element_type=jnp.float32)

def left(t, x):
    hi, lo = split(x)
    q = dot(t, jnp.concatenate([hi, lo], axis=0))
    return q[:96] + q[96:]

def right(x, w):
    hi, lo = split(x)
    o = dot(jnp.concatenate([hi, lo], axis=1), w)
    return o[:, :128] + o[:, 128:]


def transform_pairs(iv, jv, nv, fv, a_ref, k_ref, wz_ref, wi_ref, ty_ref, tyi_ref, tx_ref, point):
    lane = lax.broadcasted_iota(jnp.int32, (24 * XB, 128), 1)

    def one(t, _):
        gi = t // 2
        gj = ((t + 1) // 2) % 2
        i_ref, j_ref, near_ref, far_ref = iv.at[gi], jv.at[gj], nv.at[gi], fv.at[gj]
        near_first, far_first = gi == gj, gi == 0
        point(t, 0)

        def fwd(xb, _):
            base = xb * (XB * 72)
            d = []
            for s in range(3):
                rows = pl.ds(base + s, 24 * XB, stride=3)
                d.append(i_ref[rows, :] * j_ref[rows, :])
            m = [d[0], jnp.where(lane >= 96, d[0], d[1]), jnp.where(lane >= 64, d[1], d[2]), d[2]]
            o = [right(m[l], wz_ref[l]) for l in range(4)]
            for xx in range(0, XB, 2):
                cols = []
                for x in (xx, xx + 1):
                    cols.append(jnp.concatenate([o[l][24 * x:24 * x + 24] for l in range(4)], axis=0))
                q = left(ty_ref[...], jnp.concatenate(cols, axis=1))
                row = (xb * XB + xx) * AS
                a_ref[pl.ds(row, 96), :] = q[:, :128]
                a_ref[pl.ds(row + AS, 96), :] = q[:, 128:]
            return 0

        lax.fori_loop(0, 96 // XB, fwd, 0)
        point(t, 1)

        def mid(vb, _):
            for vv in range(0, VB, 2):
                v = vb * VB + vv
                b = jnp.concatenate([a_ref[pl.ds(v, 96, stride=AS), :], a_ref[pl.ds(v + 1, 96, stride=AS), :]], axis=1)
                kk = jnp.concatenate([k_ref[pl.ds(v * 96, 96), :], k_ref[pl.ds(v * 96 + 96, 96), :]], axis=1)
                b = left(tx_ref[...], left(tx_ref[...], b) * kk)
                a_ref[pl.ds(v, 96, stride=AS), :] = b[:, :128]
                a_ref[pl.ds(v + 1, 96, stride=AS), :] = b[:, 128:]
            return 0

        lax.fori_loop(0, 96 // VB, mid, 0)
        point(t, 2)

        def inv(xb, _):
            parts = [[] for _ in range(4)]
            for xx in range(0, XB, 2):
                row = (xb * XB + xx) * AS
                b = jnp.concatenate([a_ref[pl.ds(row, 96), :], a_ref[pl.ds(row + AS, 96), :]], axis=1)
                q = left(tyi_ref[...], b)
                for x in range(2):
                    for l in range(4):
                        parts[l].append(q[24 * l:24 * l + 24, 128 * x:128 * x + 128])
            o = [right(jnp.concatenate(parts[l], axis=0), wi_ref[l]) for l in range(4)]
            vs = [jnp.where(lane < 96, o[0], o[1]), jnp.where(lane < 64, o[1], o[2]), jnp.where(lane < 32, o[2], o[3])]
            base = xb * (XB * 72)
            for s in range(3):
                rows = pl.ds(base + s, 24 * XB, stride=3)
                near_ref[rows, :] = jnp.where(near_first, 0.0, near_ref[rows, :]) + j_ref[rows, :] * vs[s]
                far_ref[rows, :] = jnp.where(far_first, 0.0, far_ref[rows, :]) + i_ref[rows, :] * vs[s]
            return 0

        lax.fori_loop(0, 96 // XB, inv, 0)
        return 0

    lax.fori_loop(0, 4, one, 0)


MESH = pl.DeviceIdType.MESH
PIECE = 432
CHUNKS = 2
PART = PIECE // CHUNKS


class Comm:
    def __init__(self, ss, rs, some):
        self.ss, self.rs, self.some, self.sent, self.n, self.r = ss, rs, some, [], 0, 0

    def slot(self):
        self.r += 1
        return self.r - 1

    def send(self, src, dst, recv, device, when=None):
        copy = pltpu.make_async_remote_copy(src_ref=src, dst_ref=dst, send_sem=self.ss.at[self.n], recv_sem=self.rs.at[recv],
                                            device_id=device, device_id_type=MESH)
        self.n += 1
        self.sent.append((when, src.shape[0]))
        guarded(when, copy.start)

    def done(self, sem, rows):
        ref = self.some.at[pl.ds(0, rows)]
        pltpu.make_async_copy(ref, ref, sem).wait()

    def wait(self, recv, rows=PIECE):
        self.done(self.rs.at[recv], rows)

    def finish(self):
        for n, (when, rows) in enumerate(self.sent):
            guarded(when, functools.partial(self.done, self.ss.at[n], rows))


def guarded(when, do):
    if when is None:
        do()
    else:
        pl.when(when)(lambda: do())


def piece(zl, x, c):
    return pl.ds(pl.multiple_of((zl * 8 + x * 2 + c) * PIECE, PIECE), PIECE)


def chunk(zl, x, c, h):
    return pl.ds(pl.multiple_of((zl * 8 + x * 2 + c) * PIECE + h * PART, 8), PART)


def exchange(orbitals, wz_ref, wi_ref, ty_ref, tyi_ref, tx_ref, action, k_ref, planes, o, out, extra, hb, iv, jv, nv, fv, a, fw, rb, db, zb, yb, ss, rs, ls):
    fetch = [pltpu.make_async_copy(orbitals.at[b], planes.at[b], ls.at[8 + b]) for b in range(6)]
    for copy in fetch:
        copy.start()
    y, zh, zl, x, c = (lax.axis_index(n) for n in ("y", "zh", "zl", "x", "c"))
    xs = [lax.rem(x + d, 4) for d in range(4)]
    ys = [lax.rem(y + d, 4) for d in range(4)]
    own = 2 * zl + c
    quad = [(zl if k < 2 else 1 - zl, c if k % 2 == 0 else 1 - c) for k in range(4)]
    root_y, root_zh = lax.div(x, 2), lax.rem(x, 2)
    dy = lax.rem(y + 4 - root_y, 4)
    in_root_zh = zh == root_zh
    home = [in_root_zh, jnp.logical_not(in_root_zh)]
    away = [home[1], home[0]]
    prim = jnp.where(in_root_zh, zl, 1 - zl)
    band = 2 * y + zh
    gives = y < 2
    shift = lax.rem(x + 8 - band, 4)
    units = [lax.rem(x + dy + j, 4) for j in range(4)]

    def at(y=y, zh=zh, zl=zl, x=x, c=c):
        return (y, zh, zl, x, c)

    relay = [at(y=lax.rem(y + shift, 4)), at(y=lax.rem(y + shift, 4), zh=1 - zh, zl=1 - zl)]
    source = at(x=units[0], y=root_y, zh=root_zh, zl=prim)
    at_home_0 = jnp.logical_and(in_root_zh, dy == 0)
    gives_away = [jnp.logical_and(gives, shift != 0), gives]
    diagonal = lax.rem(x + 4 - y, 4)
    is_relay, passes, passed_to, passed_from = [], [], [], []
    for g in range(2):
        zr = zh if g == 0 else 1 - zh
        second = jnp.where(diagonal == zr, 0, 1)
        target = zr + 2 * second
        on_path = jnp.logical_or(diagonal == zr, diagonal == zr + 1)
        moves = jnp.logical_and(on_path, x != target)
        is_relay.append(moves if g == 0 else on_path)
        passes.append(moves)
        passed_to.append(at(x=target))
        passed_from.append(at(y=second, zh=zr, zl=zl if g == 0 else 1 - zl))
    stays = jnp.logical_and(is_relay[1], jnp.logical_not(passes[1]))
    takes = [jnp.logical_and(in_root_zh, dy != 0), home[1]]
    arrives = [takes[0], jnp.logical_and(takes[1], dy != 0)]

    barrier = pltpu.get_barrier_semaphore()
    cross = at(zh=1 - zh, zl=1 - zl)
    opposite = at(zh=1 - zh)
    friends = [at(x=xs[d]) for d in range(1, 4)] + [at(y=ys[d]) for d in range(1, 4)] + [cross, opposite]
    friends += [at(zl=qz, c=qc) for qz, qc in quad[1:]]
    for f in friends:
        pl.semaphore_signal(barrier, inc=1, device_id=f, device_id_type=MESH)
    for g in range(2):
        guarded(gives_away[g], lambda: pl.semaphore_signal(barrier, inc=1, device_id=relay[g], device_id_type=MESH))
        guarded(is_relay[g], lambda: pl.semaphore_signal(barrier, inc=1, device_id=passed_from[g], device_id_type=MESH))
    count = sum(flag.astype(jnp.int32) for flag in gives_away + is_relay)
    for copy in fetch:
        copy.wait()

    def unpack(b, _):
        for q in range(72):
            o[pl.ds(b * 72 + q, 8, stride=PIECE), :] = planes[b, :, 128 * q:128 * q + 128]
        return 0

    lax.fori_loop(0, 6, unpack, 0)
    pl.semaphore_wait(barrier, len(friends) + count)

    m = Comm(ss, rs, fw.at[0, 0, 0])

    def orbital(ref, b):
        return ref.at[pl.ds(pl.multiple_of(b * PIECE, PIECE), PIECE)]


    def slots(*shape):
        return [slots(*shape[1:]) for _ in range(shape[0])] if shape else m.slot()

    S1, S2, S3 = slots(2, 4), slots(2, 2, 4), slots(2, 2, 2)
    JA, J1, ZP, ZS = (slots(2, CHUNKS) for _ in range(4))
    YR, DIE = (slots(2, CHUNKS, 2, 4) for _ in range(2))
    kind = [prim, 1 - prim]
    keep = [pltpu.make_async_copy(orbital(o, 2 * own + g), iv.at[g, piece(zl, x, c)], ls.at[g]) for g in range(2)]
    root_keep = pltpu.make_async_copy(orbital(o, 0), jv.at[0, piece(zl, x, c)], ls.at[2])

    def i_first(g):
        for k in range(1, 4):
            qz, qc = quad[k]
            m.send(orbital(o, 2 * (2 * qz + qc) + g), iv.at[g, piece(zl, x, c)], S1[g][k], at(zl=qz, c=qc))
        keep[g].start()

    def i_spread(g, k):
        rows = piece(quad[k][0], x, quad[k][1])
        src = iv.at[g, rows]
        if k == 0:
            src = orbital(o, 2 * own + g)
        else:
            m.wait(S1[g][k])
        for d in range(2):
            m.send(src, iv.at[g, rows], S2[g][d][k], at(x=xs[1 + 2 * d]))

    def i_forward(g):
        for kk in range(2):
            for d in range(2):
                k = kk + 2 * d
                rows = iv.at[g, piece(quad[k][0], xs[3 - 2 * d], quad[k][1])]
                m.wait(S2[g][d][k])
                m.send(rows, rows, S3[g][d][kk], at(x=xs[1 + 2 * d]))

    def i_finish(g):
        keep[g].wait()
        for d in range(2):
            for kk in range(2):
                m.wait(S2[g][d][kk + 2 - 2 * d])
                m.wait(S3[g][d][kk])

    stay = [pltpu.make_async_copy(hb.at[0, 1, h], jv.at[1, chunk(prim, units[0], c, h)], ls.at[6 + h]) for h in range(2)]

    def j_first(g):
        for h in range(CHUNKS):
            m.send(orbital(o, g).at[pl.ds(h * PART, PART)], hb.at[0, g, h], JA[g][h], relay[g], gives_away[g])
        if g == 0:
            guarded(at_home_0, root_keep.start)

    def j_relay(g, h):
        guarded(is_relay[g], lambda: m.wait(JA[g][h], PART))
        m.send(hb.at[0, g, h], jv.at[g, chunk(zl if g == 0 else 1 - zl, x, c, h)], J1[g][h], passed_to[g], passes[g])
        if g == 1:
            guarded(stays, stay[h].start)

    def j_row(g, kd, h):
        rows = jv.at[g, chunk(kind[kd], units[0], c, h)]
        for j in (1, 3):
            m.send(rows, rows, YR[g][h][kd][4 - j], at(y=ys[j]))
        m.send(rows, rows, DIE[g][h][kd][0], at(c=1 - c))

    def j_entry(g, h):
        rows = jv.at[g, chunk(prim, units[0], c, h)]
        if g == 0:
            if h == 0:
                guarded(at_home_0, root_keep.wait)
        else:
            guarded(stays, stay[h].wait)
        guarded(arrives[g], lambda: m.wait(J1[g][h], PART))
        m.send(rows, rows, ZP[g][h], cross, home[g])
        m.send(rows, rows, ZS[g][h], at(zl=1 - zl), home[g])
        m.send(rows, rows, ZS[g][h], opposite, home[g])
        guarded(away[g], lambda: m.wait(ZP[g][h], PART))
        j_row(g, 0, h)

    def j_other(g, h):
        m.wait(ZS[g][h], PART)
        j_row(g, 1, h)

    def j_take(g, h, kd, j, onward=None):
        rows = jv.at[g, chunk(kind[kd], units[j], c, h)]
        m.wait(YR[g][h][kd][j], PART)
        if onward:
            m.send(rows, rows, YR[g][h][kd][2], at(y=ys[onward]))
        m.send(rows, rows, DIE[g][h][kd][j], at(c=1 - c))

    def j_pass(g):
        for kd in range(2):
            j_take(g, 0, kd, 3, 1)
            j_take(g, 1, kd, 1, 3)

    def j_rows(g):
        for kd in range(2):
            j_take(g, 0, kd, 1)
            j_take(g, 1, kd, 3)
        for kd in range(2):
            for h in range(CHUNKS):
                j_take(g, h, kd, 2)

    def j_finish(g):
        for h in range(CHUNKS):
            for kd in range(2):
                for j in range(4):
                    m.wait(DIE[g][h][kd][j], PART)

    R1, R2, R4 = slots(2, 2, 2), slots(2, 2, 4), slots(2, 4)
    put = [pltpu.make_async_copy(nv.at[g, piece(zl, x, c)], orbital(out, 2 * own + g), ls.at[3 + g]) for g in range(2)]

    through = ((2, 0), (3, 1))

    def n_first(g):
        for kk in range(2):
            for d in range(2):
                k = through[d][kk]
                m.send(nv.at[g, piece(quad[k][0], xs[2], quad[k][1])], fw.at[g, d, kk], R1[g][d][kk], at(x=xs[1 + 2 * d]))
        for kk in range(2):
            for d in range(2):
                k = through[1 - d][kk]
                m.send(nv.at[g, piece(quad[k][0], xs[1 + 2 * d], quad[k][1])], rb.at[g, d, k], R2[g][d][k], at(x=xs[1 + 2 * d]))

    def n_second(g):
        for kk in range(2):
            for d in range(2):
                k = through[d][kk]
                m.wait(R1[g][d][kk])
                rows = nv.at[g, piece(quad[k][0], xs[1 + 2 * d], quad[k][1])]
                rows[...] += fw[g, d, kk]
                m.send(rows, rb.at[g, d, k], R2[g][d][k], at(x=xs[1 + 2 * d]))

    def n_third(g):
        for k in (2, 3, 1, 0):
            rows = nv.at[g, piece(quad[k][0], x, quad[k][1])]
            m.wait(R2[g][0][k])
            m.wait(R2[g][1][k])
            rows[...] += rb[g, 0, k] + rb[g, 1, k]
            if k == 0:
                put[g].start()
            else:
                m.send(rows, orbital(out, 2 * own + g), R4[g][k], at(zl=quad[k][0], c=quad[k][1]))

    def n_finish(g):
        for k in range(1, 4):
            m.wait(R4[g][k])
        put[g].wait()

    D1, D2, D3, D5, D6 = slots(2, 2, 4), slots(2, CHUNKS, 2, 4), slots(2, CHUNKS, 3), slots(2, CHUNKS), slots(2, CHUNKS)
    root_put = pltpu.make_async_copy(fv.at[0, piece(zl, x, c)], extra.at[0], ls.at[5])

    def f_first(g):
        for j in (2, 1, 3, 0):
            for kd in range(2):
                m.send(fv.at[g, piece(kind[kd], units[j], 1 - c)], db.at[g, kd, j], D1[g][kd][j], at(c=1 - c))

    def f_second(g, h):
        part = pl.ds(h * PART, PART)
        near_j = 1 if h == 0 else 3
        for j in (2, 4 - near_j, near_j, 0):
            for kd in (1, 0):
                rows = fv.at[g, chunk(kind[kd], units[j], c, h)]
                if h == 0:
                    m.wait(D1[g][kd][j])
                rows[...] += db[g, kd, j, part]
                if j == 2:
                    m.send(rows, yb.at[g, kd, 2, part], D2[g][h][kd][2], at(y=ys[near_j]))
                if j == 4 - near_j:
                    m.send(rows, yb.at[g, kd, j, part], D2[g][h][kd][j], at(y=ys[j]))

    def f_pass(g, h):
        part = pl.ds(h * PART, PART)
        near_j = 1 if h == 0 else 3
        for kd in (1, 0):
            rows = fv.at[g, chunk(kind[kd], units[near_j], c, h)]
            m.wait(D2[g][h][kd][2], PART)
            rows[...] += yb[g, kd, 2, part]
            m.send(rows, yb.at[g, kd, near_j, part], D2[g][h][kd][near_j], at(y=ys[near_j]))

    def f_third(g, h):
        part = pl.ds(h * PART, PART)
        for kd in (1, 0):
            rows = fv.at[g, chunk(kind[kd], units[0], c, h)]
            for j in (1, 3):
                m.wait(D2[g][h][kd][j], PART)
            rows[...] += yb[g, kd, 1, part] + yb[g, kd, 3, part]
            if kd:
                m.send(rows, zb.at[g, 0, part], D3[g][h][0], at(zl=1 - zl), home[g])
                m.send(rows, zb.at[g, 1, part], D3[g][h][1], opposite, away[g])
            else:
                m.send(rows, zb.at[g, 2, part], D3[g][h][2], cross, away[g])

    def f_fourth(g, h):
        part = pl.ds(h * PART, PART)
        rows = fv.at[g, chunk(prim, units[0], c, h)]

        def go():
            for e in range(3):
                m.wait(D3[g][h][e], PART)
            rows[...] += (zb[g, 0, part] + zb[g, 1, part]) + zb[g, 2, part]

        pl.when(home[g])(go)
        if g == 0 and h == CHUNKS - 1:
            guarded(at_home_0, root_put.start)
        m.send(rows, hb.at[1, g, h], D5[g][h], at(x=units[0]), arrives[g])
        if g == 1:
            m.send(rows, extra.at[g, part], D6[g][h], source, stays)

    def f_fifth(g, h):
        guarded(passes[g], lambda: m.wait(D5[g][h], PART))
        m.send(hb.at[1, g, h], extra.at[g, pl.ds(h * PART, PART)], D6[g][h], passed_from[g], passes[g])

    def f_finish(g):
        for h in range(CHUNKS):
            guarded(gives_away[g], lambda: m.wait(D6[g][h], PART))
        if g == 0:
            guarded(at_home_0, root_put.wait)

    j_first(0)
    i_first(0)
    i_spread(0, 0)
    j_first(1)
    i_first(1)
    build_kernel(k_ref)
    for k in range(1, 4):
        i_spread(0, k)
    j_relay(0, 0)
    j_relay(0, 1)
    j_entry(0, 0)
    j_relay(1, 0)
    j_entry(0, 1)
    j_relay(1, 1)
    i_spread(1, 0)
    j_other(0, 0)
    j_entry(1, 0)
    j_other(0, 1)
    j_entry(1, 1)
    i_forward(0)
    for k in range(1, 4):
        i_spread(1, k)
    j_pass(0)
    j_other(1, 0)
    j_other(1, 1)
    j_rows(0)
    i_finish(0)
    j_pass(1)
    j_finish(0)

    def do(*steps):
        def run():
            for step in steps:
                step()

        return run

    plan = {
        (0, 1): do(lambda: i_forward(1)),
        (0, 2): do(lambda: j_rows(1)),
        (1, 0): do(lambda: j_finish(1)),
        (2, 0): do(lambda: n_first(0), lambda: i_finish(1)),
        (3, 0): do(lambda: f_first(1), lambda: n_second(0)),
        (3, 2): do(lambda: f_second(1, 0), lambda: f_second(1, 1)),
    }

    def point(t, stage):
        for (tt, ss_), run in plan.items():
            if ss_ == stage:
                pl.when(t == tt)(run)

    transform_pairs(iv, jv, nv, fv, a, k_ref, wz_ref, wi_ref, ty_ref, tyi_ref, tx_ref, point)
    n_first(1)
    f_first(0)
    f_pass(1, 0)
    f_pass(1, 1)
    f_second(0, 0)
    f_second(0, 1)
    f_third(1, 0)
    f_third(1, 1)
    n_third(0)
    n_second(1)
    f_pass(0, 0)
    f_pass(0, 1)
    f_fourth(1, 0)
    f_fourth(1, 1)
    f_third(0, 0)
    f_third(0, 1)
    f_fifth(1, 0)
    f_fifth(1, 1)
    f_fourth(0, 0)
    f_fourth(0, 1)
    f_fifth(0, 0)
    f_fifth(0, 1)
    n_third(1)
    for g in range(2):
        n_finish(g)
        f_finish(g)

    for g in range(2):

        def add():
            out[pl.ds(g * PIECE, PIECE), :] += extra[g]

        pl.when(gives)(add)

    def pack(b, _):
        for q in range(72):
            planes[b, :, 128 * q:128 * q + 128] = out[pl.ds(b * 72 + q, 8, stride=PIECE), :]
        return 0

    lax.fori_loop(0, 6, pack, 0)
    stores = [pltpu.make_async_copy(planes.at[b], action.at[b], ls.at[8 + b]) for b in range(6)]
    for store in stores:
        store.start()
    m.finish()
    for store in stores:
        store.wait()


SENDS, RECEIVES = 256, 256


def local(orbitals):
    vm = pl.BlockSpec(memory_space=pltpu.VMEM)
    an = pl.BlockSpec(memory_space=pl.ANY)
    f32 = jnp.float32
    big = pltpu.VMEM((2, 6912, 128), f32)

    def pieces(*lead):
        return pltpu.VMEM(lead + (PIECE, 128), f32)

    return pl.pallas_call(
        exchange,
        out_shape=jax.ShapeDtypeStruct((6, 8, 9216), f32),
        in_specs=[an] + [vm] * 5,
        out_specs=an,
        scratch_shapes=[pltpu.VMEM((N * N, 128), f32), pltpu.VMEM((6, 8, 9216), f32), pltpu.VMEM((8 * PIECE, 128), f32), pltpu.VMEM((8 * PIECE, 128), f32), pieces(2), pltpu.VMEM((2, 2, CHUNKS, PART, 128), f32)]
        + [big] * 4
        + [pltpu.VMEM((96 * AS, 128), f32), pieces(2, 2, 2), pieces(2, 2, 4), pieces(2, 2, 4), pieces(2, 3), pieces(2, 2, 4)]
        + [pltpu.SemaphoreType.DMA((SENDS,)), pltpu.SemaphoreType.DMA((RECEIVES,)), pltpu.SemaphoreType.DMA((16,))],
        compiler_params=pltpu.CompilerParams(vmem_limit_bytes=67043328, collective_id=1, has_side_effects=True),
    )(orbitals.transpose(1, 0, 2), *tables()).transpose(1, 0, 2)


def solution(mesh):
    fine = jax.sharding.Mesh(mesh.devices.reshape(4, 2, 2, 4, 2), ("y", "zh", "zl", "x", "c"))
    placed = P(("y", "zh"), ("zl", "x", "c"), None)
    return jax.shard_map(local, mesh=fine, in_specs=(placed,), out_specs=placed, check_vma=False)
```

```python
import math, functools
import numpy as np
import jax, jax.numpy as jnp
from jax import lax
from jax.experimental import pallas as pl
from jax.experimental.pallas import tpu as pltpu
from jax.sharding import PartitionSpec as P
import ml_dtypes

N = 96
OMEGA = 0.106
CELL = 41.05
bf = jnp.bfloat16
XB, VB, AS = 32, 32, 97

def split_np(t):
    t = t.astype(np.float32)
    hi = t.astype(ml_dtypes.bfloat16)
    lo = (t - hi.astype(np.float32)).astype(ml_dtypes.bfloat16)
    return hi, lo

def tables():
    k = np.arange(N)
    ang = 2*np.pi*((k[:,None]*k[None,:])%N)/N
    T = np.cos(ang)+np.sin(ang)
    hi, lo = split_np(T)
    wz = np.zeros((4,256,256), ml_dtypes.bfloat16)
    wi = np.zeros((4,256,256), ml_dtypes.bfloat16)
    for l in range(4):
        lane = (96*l + np.arange(N)) % 128
        wz[l, lane, 0:96] = hi
        wz[l, lane, 128:224] = lo
        wz[l, 128+lane, 0:96] = hi
        wi[l, 0:96, lane] = hi.T
        wi[l, 0:96, 128+lane] = lo.T
        wi[l, 128:224, lane] = hi.T
    def two(hi, lo):
        t = np.zeros((192,192), ml_dtypes.bfloat16)
        t[:96,:96]=hi; t[:96,96:]=hi; t[96:,:96]=lo
        return t
    order = np.array([4*kk+l for l in range(4) for kk in range(24)])
    ty = two(hi[:,order], lo[:,order])
    tyi = two(hi[order,:], lo[order,:])
    tx = two(hi, lo)
    return wz, wi, ty, tyi, tx

def build_kernel(k_ref):
    def square(index):
        index = index.astype(jnp.float32)
        freq = jnp.where(index <= N // 2, index, index - N)
        return freq * freq

    u = square(lax.broadcasted_iota(jnp.int32, (N, 128), 0))
    w = square(jnp.minimum(lax.broadcasted_iota(jnp.int32, (N, 128), 1), N - 1))
    plane = u + w
    scale = (2.0 * math.pi / CELL) ** 2
    factor = -0.25 / float(N**3)

    def one(v, _):
        g_two = scale * (plane + square(v))
        positive = g_two > 0
        safe = jnp.where(positive, g_two, 1.0)
        value = (4.0 * math.pi * factor) / safe * (1.0 - jnp.exp(safe * (-1.0 / (4.0 * OMEGA * OMEGA))))
        k_ref[pl.ds(pl.multiple_of(v * N, 8), N), :] = jnp.where(positive, value, math.pi / (OMEGA * OMEGA) * factor)
        return 0

    lax.fori_loop(0, N, one, 0)


def split(x):
    hi = x.astype(bf)
    lo = (x - hi.astype(jnp.float32)).astype(bf)
    return hi, lo

def dot(a, b):
    return lax.dot_general(a, b, (((1,),(0,)),((),())), preferred_element_type=jnp.float32)

def left(t, x):
    hi, lo = split(x)
    q = dot(t, jnp.concatenate([hi, lo], axis=0))
    return q[:96] + q[96:]

def right(x, w):
    hi, lo = split(x)
    o = dot(jnp.concatenate([hi, lo], axis=1), w)
    return o[:, :128] + o[:, 128:]


def transform_pairs(iv, jv, nv, fv, a_ref, k_ref, wz_ref, wi_ref, ty_ref, tyi_ref, tx_ref, point):
    lane = lax.broadcasted_iota(jnp.int32, (24 * XB, 128), 1)

    def one(t, _):
        gi = t // 2
        gj = ((t + 1) // 2) % 2
        i_ref, j_ref, near_ref, far_ref = iv.at[gi], jv.at[gj], nv.at[gi], fv.at[gj]
        near_first, far_first = gi == gj, gi == 0
        point(t, 0)

        def fwd(xb, _):
            base = xb * (XB * 72)
            d = []
            for s in range(3):
                rows = pl.ds(base + s, 24 * XB, stride=3)
                d.append(i_ref[rows, :] * j_ref[rows, :])
            m = [d[0], jnp.where(lane >= 96, d[0], d[1]), jnp.where(lane >= 64, d[1], d[2]), d[2]]
            o = [right(m[l], wz_ref[l]) for l in range(4)]
            for xx in range(0, XB, 2):
                cols = []
                for x in (xx, xx + 1):
                    cols.append(jnp.concatenate([o[l][24 * x:24 * x + 24] for l in range(4)], axis=0))
                q = left(ty_ref[...], jnp.concatenate(cols, axis=1))
                row = (xb * XB + xx) * AS
                a_ref[pl.ds(row, 96), :] = q[:, :128]
                a_ref[pl.ds(row + AS, 96), :] = q[:, 128:]
            return 0

        lax.fori_loop(0, 96 // XB, fwd, 0)
        point(t, 1)

        def mid(vb, _):
            for vv in range(0, VB, 2):
                v = vb * VB + vv
                b = jnp.concatenate([a_ref[pl.ds(v, 96, stride=AS), :], a_ref[pl.ds(v + 1, 96, stride=AS), :]], axis=1)
                kk = jnp.concatenate([k_ref[pl.ds(v * 96, 96), :], k_ref[pl.ds(v * 96 + 96, 96), :]], axis=1)
                b = left(tx_ref[...], left(tx_ref[...], b) * kk)
                a_ref[pl.ds(v, 96, stride=AS), :] = b[:, :128]
                a_ref[pl.ds(v + 1, 96, stride=AS), :] = b[:, 128:]
            return 0

        lax.fori_loop(0, 96 // VB, mid, 0)
        point(t, 2)

        def inv(xb, _):
            parts = [[] for _ in range(4)]
            for xx in range(0, XB, 2):
                row = (xb * XB + xx) * AS
                b = jnp.concatenate([a_ref[pl.ds(row, 96), :], a_ref[pl.ds(row + AS, 96), :]], axis=1)
                q = left(tyi_ref[...], b)
                for x in range(2):
                    for l in range(4):
                        parts[l].append(q[24 * l:24 * l + 24, 128 * x:128 * x + 128])
            o = [right(jnp.concatenate(parts[l], axis=0), wi_ref[l]) for l in range(4)]
            vs = [jnp.where(lane < 96, o[0], o[1]), jnp.where(lane < 64, o[1], o[2]), jnp.where(lane < 32, o[2], o[3])]
            base = xb * (XB * 72)
            for s in range(3):
                rows = pl.ds(base + s, 24 * XB, stride=3)
                near_ref[rows, :] = jnp.where(near_first, 0.0, near_ref[rows, :]) + j_ref[rows, :] * vs[s]
                far_ref[rows, :] = jnp.where(far_first, 0.0, far_ref[rows, :]) + i_ref[rows, :] * vs[s]
            return 0

        lax.fori_loop(0, 96 // XB, inv, 0)
        return 0

    lax.fori_loop(0, 4, one, 0)


MESH = pl.DeviceIdType.MESH
PIECE = 432
CHUNKS = 2
PART = PIECE // CHUNKS


class Comm:
    def __init__(self, ss, rs, some):
        self.ss, self.rs, self.some, self.sent, self.n, self.r = ss, rs, some, [], 0, 0

    def slot(self):
        self.r += 1
        return self.r - 1

    def send(self, src, dst, recv, device, when=None):
        copy = pltpu.make_async_remote_copy(src_ref=src, dst_ref=dst, send_sem=self.ss.at[self.n], recv_sem=self.rs.at[recv],
                                            device_id=device, device_id_type=MESH)
        self.n += 1
        self.sent.append((when, src.shape[0]))
        guarded(when, copy.start)

    def done(self, sem, rows):
        ref = self.some.at[pl.ds(0, rows)]
        pltpu.make_async_copy(ref, ref, sem).wait()

    def wait(self, recv, rows=PIECE):
        self.done(self.rs.at[recv], rows)

    def finish(self):
        for n, (when, rows) in enumerate(self.sent):
            guarded(when, functools.partial(self.done, self.ss.at[n], rows))


def guarded(when, do):
    if when is None:
        do()
    else:
        pl.when(when)(lambda: do())


def piece(zl, x, c):
    return pl.ds(pl.multiple_of((zl * 8 + x * 2 + c) * PIECE, PIECE), PIECE)


def chunk(zl, x, c, h):
    return pl.ds(pl.multiple_of((zl * 8 + x * 2 + c) * PIECE + h * PART, 8), PART)


def exchange(orbitals, wz_ref, wi_ref, ty_ref, tyi_ref, tx_ref, action, k_ref, planes, o, out, extra, hb, iv, jv, nv, fv, a, fw, rb, db, zb, yb, ss, rs, ls):
    fetch = [pltpu.make_async_copy(orbitals.at[b], planes.at[b], ls.at[8 + b]) for b in range(6)]
    for copy in fetch:
        copy.start()
    y, zh, zl, x, c = (lax.axis_index(n) for n in ("y", "zh", "zl", "x", "c"))
    xs = [lax.rem(x + d, 4) for d in range(4)]
    ys = [lax.rem(y + d, 4) for d in range(4)]
    own = 2 * zl + c
    quad = [(zl if k < 2 else 1 - zl, c if k % 2 == 0 else 1 - c) for k in range(4)]
    root_y, root_zh = lax.div(x, 2), lax.rem(x, 2)
    dy = lax.rem(y + 4 - root_y, 4)
    in_root_zh = zh == root_zh
    home = [in_root_zh, jnp.logical_not(in_root_zh)]
    away = [home[1], home[0]]
    prim = jnp.where(in_root_zh, zl, 1 - zl)
    band = 2 * y + zh
    gives = y < 2
    shift = lax.rem(x + 8 - band, 4)
    units = [lax.rem(x + dy + j, 4) for j in range(4)]

    def at(y=y, zh=zh, zl=zl, x=x, c=c):
        return (y, zh, zl, x, c)

    relay = [at(y=lax.rem(y + shift, 4)), at(y=lax.rem(y + shift, 4), zh=1 - zh, zl=1 - zl)]
    source = at(x=units[0], y=root_y, zh=root_zh, zl=prim)
    at_home_0 = jnp.logical_and(in_root_zh, dy == 0)
    gives_away = [jnp.logical_and(gives, shift != 0), gives]
    diagonal = lax.rem(x + 4 - y, 4)
    is_relay, passes, passed_to, passed_from = [], [], [], []
    for g in range(2):
        zr = zh if g == 0 else 1 - zh
        second = jnp.where(diagonal == zr, 0, 1)
        target = zr + 2 * second
        on_path = jnp.logical_or(diagonal == zr, diagonal == zr + 1)
        moves = jnp.logical_and(on_path, x != target)
        is_relay.append(moves if g == 0 else on_path)
        passes.append(moves)
        passed_to.append(at(x=target))
        passed_from.append(at(y=second, zh=zr, zl=zl if g == 0 else 1 - zl))
    stays = jnp.logical_and(is_relay[1], jnp.logical_not(passes[1]))
    takes = [jnp.logical_and(in_root_zh, dy != 0), home[1]]
    arrives = [takes[0], jnp.logical_and(takes[1], dy != 0)]

    barrier = pltpu.get_barrier_semaphore()
    cross = at(zh=1 - zh, zl=1 - zl)
    opposite = at(zh=1 - zh)
    friends = [at(x=xs[d]) for d in range(1, 4)] + [at(y=ys[d]) for d in range(1, 4)] + [cross, opposite]
    friends += [at(zl=qz, c=qc) for qz, qc in quad[1:]]
    for f in friends:
        pl.semaphore_signal(barrier, inc=1, device_id=f, device_id_type=MESH)
    for g in range(2):
        guarded(gives_away[g], lambda: pl.semaphore_signal(barrier, inc=1, device_id=relay[g], device_id_type=MESH))
        guarded(is_relay[g], lambda: pl.semaphore_signal(barrier, inc=1, device_id=passed_from[g], device_id_type=MESH))
    count = sum(flag.astype(jnp.int32) for flag in gives_away + is_relay)
    for copy in fetch:
        copy.wait()

    def unpack(b, _):
        for q in range(72):
            o[pl.ds(b * 72 + q, 8, stride=PIECE), :] = planes[b, :, 128 * q:128 * q + 128]
        return 0

    lax.fori_loop(0, 6, unpack, 0)
    pl.semaphore_wait(barrier, len(friends) + count)

    m = Comm(ss, rs, fw.at[0, 0, 0])

    def orbital(ref, b):
        return ref.at[pl.ds(pl.multiple_of(b * PIECE, PIECE), PIECE)]


    def slots(*shape):
        return [slots(*shape[1:]) for _ in range(shape[0])] if shape else m.slot()

    S1, S2, S3 = slots(2, 4), slots(2, 2, 4), slots(2, 2, 2)
    JA, J1, ZP, ZS = (slots(2, CHUNKS) for _ in range(4))
    YR, DIE = (slots(2, CHUNKS, 2, 4) for _ in range(2))
    kind = [prim, 1 - prim]
    keep = [pltpu.make_async_copy(orbital(o, 2 * own + g), iv.at[g, piece(zl, x, c)], ls.at[g]) for g in range(2)]
    root_keep = pltpu.make_async_copy(orbital(o, 0), jv.at[0, piece(zl, x, c)], ls.at[2])

    def i_first(g):
        for k in range(1, 4):
            qz, qc = quad[k]
            m.send(orbital(o, 2 * (2 * qz + qc) + g), iv.at[g, piece(zl, x, c)], S1[g][k], at(zl=qz, c=qc))
        keep[g].start()

    def i_spread(g, k):
        rows = piece(quad[k][0], x, quad[k][1])
        src = iv.at[g, rows]
        if k == 0:
            src = orbital(o, 2 * own + g)
        else:
            m.wait(S1[g][k])
        for d in range(2):
            m.send(src, iv.at[g, rows], S2[g][d][k], at(x=xs[1 + 2 * d]))

    def i_forward(g):
        for kk in range(2):
            for d in range(2):
                k = kk + 2 * d
                rows = iv.at[g, piece(quad[k][0], xs[3 - 2 * d], quad[k][1])]
                m.wait(S2[g][d][k])
                m.send(rows, rows, S3[g][d][kk], at(x=xs[1 + 2 * d]))

    def i_finish(g):
        keep[g].wait()
        for d in range(2):
            for kk in range(2):
                m.wait(S2[g][d][kk + 2 - 2 * d])
                m.wait(S3[g][d][kk])

    stay = [pltpu.make_async_copy(hb.at[0, 1, h], jv.at[1, chunk(prim, units[0], c, h)], ls.at[6 + h]) for h in range(2)]

    def j_first(g):
        for h in range(CHUNKS):
            m.send(orbital(o, g).at[pl.ds(h * PART, PART)], hb.at[0, g, h], JA[g][h], relay[g], gives_away[g])
        if g == 0:
            guarded(at_home_0, root_keep.start)

    def j_relay(g, h):
        guarded(is_relay[g], lambda: m.wait(JA[g][h], PART))
        m.send(hb.at[0, g, h], jv.at[g, chunk(zl if g == 0 else 1 - zl, x, c, h)], J1[g][h], passed_to[g], passes[g])
        if g == 1:
            guarded(stays, stay[h].start)

    def j_row(g, kd, h):
        rows = jv.at[g, chunk(kind[kd], units[0], c, h)]
        for j in (1, 3):
            m.send(rows, rows, YR[g][h][kd][4 - j], at(y=ys[j]))
        m.send(rows, rows, DIE[g][h][kd][0], at(c=1 - c))

    def j_entry(g, h):
        rows = jv.at[g, chunk(prim, units[0], c, h)]
        if g == 0:
            if h == 0:
                guarded(at_home_0, root_keep.wait)
        else:
            guarded(stays, stay[h].wait)
        guarded(arrives[g], lambda: m.wait(J1[g][h], PART))
        m.send(rows, rows, ZP[g][h], cross, home[g])
        m.send(rows, rows, ZS[g][h], at(zl=1 - zl), home[g])
        m.send(rows, rows, ZS[g][h], opposite, home[g])
        guarded(away[g], lambda: m.wait(ZP[g][h], PART))
        j_row(g, 0, h)

    def j_other(g, h):
        m.wait(ZS[g][h], PART)
        j_row(g, 1, h)

    def j_take(g, h, kd, j, onward=None):
        rows = jv.at[g, chunk(kind[kd], units[j], c, h)]
        m.wait(YR[g][h][kd][j], PART)
        if onward:
            m.send(rows, rows, YR[g][h][kd][2], at(y=ys[onward]))
        m.send(rows, rows, DIE[g][h][kd][j], at(c=1 - c))

    def j_pass(g):
        for kd in range(2):
            j_take(g, 0, kd, 3, 1)
            j_take(g, 1, kd, 1, 3)

    def j_rows(g):
        for kd in range(2):
            j_take(g, 0, kd, 1)
            j_take(g, 1, kd, 3)
        for kd in range(2):
            for h in range(CHUNKS):
                j_take(g, h, kd, 2)

    def j_finish(g):
        for h in range(CHUNKS):
            for kd in range(2):
                for j in range(4):
                    m.wait(DIE[g][h][kd][j], PART)

    R1, R2, R4 = slots(2, 2, 2), slots(2, 2, 4), slots(2, 4)
    put = [pltpu.make_async_copy(nv.at[g, piece(zl, x, c)], orbital(out, 2 * own + g), ls.at[3 + g]) for g in range(2)]

    through = ((2, 0), (3, 1))

    def n_first(g):
        for kk in range(2):
            for d in range(2):
                k = through[d][kk]
                m.send(nv.at[g, piece(quad[k][0], xs[2], quad[k][1])], fw.at[g, d, kk], R1[g][d][kk], at(x=xs[1 + 2 * d]))
        for kk in range(2):
            for d in range(2):
                k = through[1 - d][kk]
                m.send(nv.at[g, piece(quad[k][0], xs[1 + 2 * d], quad[k][1])], rb.at[g, d, k], R2[g][d][k], at(x=xs[1 + 2 * d]))

    def n_second(g):
        for kk in range(2):
            for d in range(2):
                k = through[d][kk]
                m.wait(R1[g][d][kk])
                rows = nv.at[g, piece(quad[k][0], xs[1 + 2 * d], quad[k][1])]
                rows[...] += fw[g, d, kk]
                m.send(rows, rb.at[g, d, k], R2[g][d][k], at(x=xs[1 + 2 * d]))

    def n_third(g):
        for k in (2, 3, 1, 0):
            rows = nv.at[g, piece(quad[k][0], x, quad[k][1])]
            m.wait(R2[g][0][k])
            m.wait(R2[g][1][k])
            rows[...] += rb[g, 0, k] + rb[g, 1, k]
            if k == 0:
                put[g].start()
            else:
                m.send(rows, orbital(out, 2 * own + g), R4[g][k], at(zl=quad[k][0], c=quad[k][1]))

    def n_finish(g):
        for k in range(1, 4):
            m.wait(R4[g][k])
        put[g].wait()

    D1, D2, D3, D5, D6 = slots(2, 2, 4), slots(2, CHUNKS, 2, 4), slots(2, CHUNKS, 3), slots(2, CHUNKS), slots(2, CHUNKS)
    root_put = pltpu.make_async_copy(fv.at[0, piece(zl, x, c)], extra.at[0], ls.at[5])

    def f_first(g):
        for j in (2, 1, 3, 0):
            for kd in range(2):
                m.send(fv.at[g, piece(kind[kd], units[j], 1 - c)], db.at[g, kd, j], D1[g][kd][j], at(c=1 - c))

    def f_second(g, h):
        part = pl.ds(h * PART, PART)
        near_j = 1 if h == 0 else 3
        for j in (2, 4 - near_j, near_j, 0):
            for kd in (1, 0):
                rows = fv.at[g, chunk(kind[kd], units[j], c, h)]
                if h == 0:
                    m.wait(D1[g][kd][j])
                rows[...] += db[g, kd, j, part]
                if j == 2:
                    m.send(rows, yb.at[g, kd, 2, part], D2[g][h][kd][2], at(y=ys[near_j]))
                if j == 4 - near_j:
                    m.send(rows, yb.at[g, kd, j, part], D2[g][h][kd][j], at(y=ys[j]))

    def f_pass(g, h):
        part = pl.ds(h * PART, PART)
        near_j = 1 if h == 0 else 3
        for kd in (1, 0):
            rows = fv.at[g, chunk(kind[kd], units[near_j], c, h)]
            m.wait(D2[g][h][kd][2], PART)
            rows[...] += yb[g, kd, 2, part]
            m.send(rows, yb.at[g, kd, near_j, part], D2[g][h][kd][near_j], at(y=ys[near_j]))

    def f_third(g, h):
        part = pl.ds(h * PART, PART)
        for kd in (1, 0):
            rows = fv.at[g, chunk(kind[kd], units[0], c, h)]
            for j in (1, 3):
                m.wait(D2[g][h][kd][j], PART)
            rows[...] += yb[g, kd, 1, part] + yb[g, kd, 3, part]
            if kd:
                m.send(rows, zb.at[g, 0, part], D3[g][h][0], at(zl=1 - zl), home[g])
                m.send(rows, zb.at[g, 1, part], D3[g][h][1], opposite, away[g])
            else:
                m.send(rows, zb.at[g, 2, part], D3[g][h][2], cross, away[g])

    def f_fourth(g, h):
        part = pl.ds(h * PART, PART)
        rows = fv.at[g, chunk(prim, units[0], c, h)]

        def go():
            for e in range(3):
                m.wait(D3[g][h][e], PART)
            rows[...] += (zb[g, 0, part] + zb[g, 1, part]) + zb[g, 2, part]

        pl.when(home[g])(go)
        if g == 0 and h == CHUNKS - 1:
            guarded(at_home_0, root_put.start)
        m.send(rows, hb.at[1, g, h], D5[g][h], at(x=units[0]), arrives[g])
        if g == 1:
            m.send(rows, extra.at[g, part], D6[g][h], source, stays)

    def f_fifth(g, h):
        guarded(passes[g], lambda: m.wait(D5[g][h], PART))
        m.send(hb.at[1, g, h], extra.at[g, pl.ds(h * PART, PART)], D6[g][h], passed_from[g], passes[g])

    def f_finish(g):
        for h in range(CHUNKS):
            guarded(gives_away[g], lambda: m.wait(D6[g][h], PART))
        if g == 0:
            guarded(at_home_0, root_put.wait)

    j_first(0)
    i_first(0)
    i_spread(0, 0)
    j_first(1)
    i_first(1)
    build_kernel(k_ref)
    for k in range(1, 4):
        i_spread(0, k)
    j_relay(0, 0)
    j_relay(0, 1)
    j_entry(0, 0)
    j_relay(1, 0)
    j_entry(0, 1)
    j_relay(1, 1)
    i_spread(1, 0)
    j_other(0, 0)
    j_entry(1, 0)
    j_other(0, 1)
    j_entry(1, 1)
    i_forward(0)
    for k in range(1, 4):
        i_spread(1, k)
    j_pass(0)
    j_other(1, 0)
    j_other(1, 1)
    j_rows(0)
    i_finish(0)
    j_pass(1)
    j_finish(0)

    def do(*steps):
        def run():
            for step in steps:
                step()

        return run

    plan = {
        (0, 1): do(lambda: i_forward(1)),
        (0, 2): do(lambda: j_rows(1)),
        (1, 0): do(lambda: j_finish(1)),
        (2, 0): do(lambda: n_first(0), lambda: i_finish(1)),
        (3, 0): do(lambda: f_first(1), lambda: n_second(0)),
        (3, 2): do(lambda: f_second(1, 0), lambda: f_second(1, 1)),
    }

    def point(t, stage):
        for (tt, ss_), run in plan.items():
            if ss_ == stage:
                pl.when(t == tt)(run)

    transform_pairs(iv, jv, nv, fv, a, k_ref, wz_ref, wi_ref, ty_ref, tyi_ref, tx_ref, point)
    n_first(1)
    f_first(0)
    f_pass(1, 0)
    f_pass(1, 1)
    f_second(0, 0)
    f_second(0, 1)
    f_third(1, 0)
    f_third(1, 1)
    n_third(0)
    n_second(1)
    f_pass(0, 0)
    f_pass(0, 1)
    f_fourth(1, 0)
    f_fourth(1, 1)
    f_third(0, 0)
    f_third(0, 1)
    f_fifth(1, 0)
    f_fifth(1, 1)
    f_fourth(0, 0)
    f_fourth(0, 1)
    f_fifth(0, 0)
    f_fifth(0, 1)
    n_third(1)
    for g in range(2):
        n_finish(g)
        f_finish(g)

    for g in range(2):

        def add():
            out[pl.ds(g * PIECE, PIECE), :] += extra[g]

        pl.when(gives)(add)

    def pack(b, _):
        for q in range(72):
            planes[b, :, 128 * q:128 * q + 128] = out[pl.ds(b * 72 + q, 8, stride=PIECE), :]
        return 0

    lax.fori_loop(0, 6, pack, 0)
    stores = [pltpu.make_async_copy(planes.at[b], action.at[b], ls.at[8 + b]) for b in range(6)]
    for store in stores:
        store.start()
    m.finish()
    for store in stores:
        store.wait()


SENDS, RECEIVES = 256, 256


def local(orbitals):
    vm = pl.BlockSpec(memory_space=pltpu.VMEM)
    an = pl.BlockSpec(memory_space=pl.ANY)
    f32 = jnp.float32
    big = pltpu.VMEM((2, 6912, 128), f32)

    def pieces(*lead):
        return pltpu.VMEM(lead + (PIECE, 128), f32)

    return pl.pallas_call(
        exchange,
        out_shape=jax.ShapeDtypeStruct((6, 8, 9216), f32),
        in_specs=[an] + [vm] * 5,
        out_specs=an,
        scratch_shapes=[pltpu.VMEM((N * N, 128), f32), pltpu.VMEM((6, 8, 9216), f32), pltpu.VMEM((8 * PIECE, 128), f32), pltpu.VMEM((8 * PIECE, 128), f32), pieces(2), pltpu.VMEM((2, 2, CHUNKS, PART, 128), f32)]
        + [big] * 4
        + [pltpu.VMEM((96 * AS, 128), f32), pieces(2, 2, 2), pieces(2, 2, 4), pieces(2, 2, 4), pieces(2, 3), pieces(2, 2, 4)]
        + [pltpu.SemaphoreType.DMA((SENDS,)), pltpu.SemaphoreType.DMA((RECEIVES,)), pltpu.SemaphoreType.DMA((16,))],
        compiler_params=pltpu.CompilerParams(vmem_limit_bytes=67043328, collective_id=1, has_side_effects=True),
    )(orbitals.transpose(1, 0, 2), *tables()).transpose(1, 0, 2)


def solution(mesh):
    fine = jax.sharding.Mesh(mesh.devices.reshape(4, 2, 2, 4, 2), ("y", "zh", "zl", "x", "c"))
    placed = P(("y", "zh"), ("zl", "x", "c"), None)
    return jax.shard_map(local, mesh=fine, in_specs=(placed,), out_specs=placed, check_vma=False)
```

```python
import math, functools
import numpy as np
import jax, jax.numpy as jnp
from jax import lax
from jax.experimental import pallas as pl
from jax.experimental.pallas import tpu as pltpu
from jax.sharding import PartitionSpec as P
import ml_dtypes

N = 96
OMEGA = 0.106
CELL = 41.05
bf = jnp.bfloat16
XB, VB, AS = 32, 48, 97

def split_np(t):
    t = t.astype(np.float32)
    hi = t.astype(ml_dtypes.bfloat16)
    lo = (t - hi.astype(np.float32)).astype(ml_dtypes.bfloat16)
    return hi, lo

def tables():
    k = np.arange(N)
    ang = 2*np.pi*((k[:,None]*k[None,:])%N)/N
    T = np.cos(ang)+np.sin(ang)
    hi, lo = split_np(T)
    wz = np.zeros((4,256,256), ml_dtypes.bfloat16)
    wi = np.zeros((4,256,256), ml_dtypes.bfloat16)
    for l in range(4):
        lane = (96*l + np.arange(N)) % 128
        wz[l, lane, 0:96] = hi
        wz[l, lane, 128:224] = lo
        wz[l, 128+lane, 0:96] = hi
        wi[l, 0:96, lane] = hi.T
        wi[l, 0:96, 128+lane] = lo.T
        wi[l, 128:224, lane] = hi.T
    def two(hi, lo):
        t = np.zeros((192,192), ml_dtypes.bfloat16)
        t[:96,:96]=hi; t[:96,96:]=hi; t[96:,:96]=lo
        return t
    order = np.array([4*kk+l for l in range(4) for kk in range(24)])
    ty = two(hi[:,order], lo[:,order])
    tyi = two(hi[order,:], lo[order,:])
    tx = two(hi, lo)
    return wz, wi, ty, tyi, tx

def build_kernel(k_ref):
    def square(index):
        index = index.astype(jnp.float32)
        freq = jnp.where(index <= N // 2, index, index - N)
        return freq * freq

    u = square(lax.broadcasted_iota(jnp.int32, (N, 128), 0))
    w = square(jnp.minimum(lax.broadcasted_iota(jnp.int32, (N, 128), 1), N - 1))
    plane = u + w
    scale = (2.0 * math.pi / CELL) ** 2
    factor = -0.25 / float(N**3)

    def one(v, _):
        g_two = scale * (plane + square(v))
        positive = g_two > 0
        safe = jnp.where(positive, g_two, 1.0)
        value = (4.0 * math.pi * factor) / safe * (1.0 - jnp.exp(safe * (-1.0 / (4.0 * OMEGA * OMEGA))))
        k_ref[pl.ds(pl.multiple_of(v * N, 8), N), :] = jnp.where(positive, value, math.pi / (OMEGA * OMEGA) * factor)
        return 0

    lax.fori_loop(0, N, one, 0)


def split(x):
    hi = x.astype(bf)
    lo = (x - hi.astype(jnp.float32)).astype(bf)
    return hi, lo

def dot(a, b):
    return lax.dot_general(a, b, (((1,),(0,)),((),())), preferred_element_type=jnp.float32)

def left(t, x):
    hi, lo = split(x)
    q = dot(t, jnp.concatenate([hi, lo], axis=0))
    return q[:96] + q[96:]

def right(x, w):
    hi, lo = split(x)
    o = dot(jnp.concatenate([hi, lo], axis=1), w)
    return o[:, :128] + o[:, 128:]


def transform_pairs(iv, jv, nv, fv, a_ref, k_ref, wz_ref, wi_ref, ty_ref, tyi_ref, tx_ref, point):
    lane = lax.broadcasted_iota(jnp.int32, (24 * XB, 128), 1)

    def one(t, _):
        gi = t // 2
        gj = ((t + 1) // 2) % 2
        i_ref, j_ref, near_ref, far_ref = iv.at[gi], jv.at[gj], nv.at[gi], fv.at[gj]
        near_first, far_first = gi == gj, gi == 0
        point(t, 0)

        def fwd(xb, _):
            base = xb * (XB * 72)
            d = []
            for s in range(3):
                rows = pl.ds(base + s, 24 * XB, stride=3)
                d.append(i_ref[rows, :] * j_ref[rows, :])
            m = [d[0], jnp.where(lane >= 96, d[0], d[1]), jnp.where(lane >= 64, d[1], d[2]), d[2]]
            o = [right(m[l], wz_ref[l]) for l in range(4)]
            for xx in range(0, XB, 2):
                cols = []
                for x in (xx, xx + 1):
                    cols.append(jnp.concatenate([o[l][24 * x:24 * x + 24] for l in range(4)], axis=0))
                q = left(ty_ref[...], jnp.concatenate(cols, axis=1))
                row = (xb * XB + xx) * AS
                a_ref[pl.ds(row, 96), :] = q[:, :128]
                a_ref[pl.ds(row + AS, 96), :] = q[:, 128:]
            return 0

        lax.fori_loop(0, 96 // XB, fwd, 0)
        point(t, 1)

        def mid(vb, _):
            for vv in range(0, VB, 2):
                v = vb * VB + vv
                b = jnp.concatenate([a_ref[pl.ds(v, 96, stride=AS), :], a_ref[pl.ds(v + 1, 96, stride=AS), :]], axis=1)
                kk = jnp.concatenate([k_ref[pl.ds(v * 96, 96), :], k_ref[pl.ds(v * 96 + 96, 96), :]], axis=1)
                b = left(tx_ref[...], left(tx_ref[...], b) * kk)
                a_ref[pl.ds(v, 96, stride=AS), :] = b[:, :128]
                a_ref[pl.ds(v + 1, 96, stride=AS), :] = b[:, 128:]
            return 0

        lax.fori_loop(0, 96 // VB, mid, 0)
        point(t, 2)

        def inv(xb, _):
            parts = [[] for _ in range(4)]
            for xx in range(0, XB, 2):
                row = (xb * XB + xx) * AS
                b = jnp.concatenate([a_ref[pl.ds(row, 96), :], a_ref[pl.ds(row + AS, 96), :]], axis=1)
                q = left(tyi_ref[...], b)
                for x in range(2):
                    for l in range(4):
                        parts[l].append(q[24 * l:24 * l + 24, 128 * x:128 * x + 128])
            o = [right(jnp.concatenate(parts[l], axis=0), wi_ref[l]) for l in range(4)]
            vs = [jnp.where(lane < 96, o[0], o[1]), jnp.where(lane < 64, o[1], o[2]), jnp.where(lane < 32, o[2], o[3])]
            base = xb * (XB * 72)
            for s in range(3):
                rows = pl.ds(base + s, 24 * XB, stride=3)
                near_ref[rows, :] = jnp.where(near_first, 0.0, near_ref[rows, :]) + j_ref[rows, :] * vs[s]
                far_ref[rows, :] = jnp.where(far_first, 0.0, far_ref[rows, :]) + i_ref[rows, :] * vs[s]
            return 0

        lax.fori_loop(0, 96 // XB, inv, 0)
        return 0

    lax.fori_loop(0, 4, one, 0)


MESH = pl.DeviceIdType.MESH
PIECE = 432
CHUNKS = 2
PART = PIECE // CHUNKS


class Comm:
    def __init__(self, ss, rs, some):
        self.ss, self.rs, self.some, self.sent, self.n, self.r = ss, rs, some, [], 0, 0

    def slot(self):
        self.r += 1
        return self.r - 1

    def send(self, src, dst, recv, device, when=None):
        copy = pltpu.make_async_remote_copy(src_ref=src, dst_ref=dst, send_sem=self.ss.at[self.n], recv_sem=self.rs.at[recv],
                                            device_id=device, device_id_type=MESH)
        self.n += 1
        self.sent.append((when, src.shape[0]))
        guarded(when, copy.start)

    def done(self, sem, rows):
        ref = self.some.at[pl.ds(0, rows)]
        pltpu.make_async_copy(ref, ref, sem).wait()

    def wait(self, recv, rows=PIECE):
        self.done(self.rs.at[recv], rows)

    def finish(self):
        for n, (when, rows) in enumerate(self.sent):
            guarded(when, functools.partial(self.done, self.ss.at[n], rows))


def guarded(when, do):
    if when is None:
        do()
    else:
        pl.when(when)(lambda: do())


def piece(zl, x, c):
    return pl.ds(pl.multiple_of((zl * 8 + x * 2 + c) * PIECE, PIECE), PIECE)


def chunk(zl, x, c, h):
    return pl.ds(pl.multiple_of((zl * 8 + x * 2 + c) * PIECE + h * PART, 8), PART)


def exchange(orbitals, wz_ref, wi_ref, ty_ref, tyi_ref, tx_ref, action, k_ref, planes, o, out, extra, hb, iv, jv, nv, fv, a, fw, rb, db, zb, yb, ss, rs, ls):
    fetch = [pltpu.make_async_copy(orbitals.at[b], planes.at[b], ls.at[8 + b]) for b in range(6)]
    for copy in fetch:
        copy.start()
    y, zh, zl, x, c = (lax.axis_index(n) for n in ("y", "zh", "zl", "x", "c"))
    xs = [lax.rem(x + d, 4) for d in range(4)]
    ys = [lax.rem(y + d, 4) for d in range(4)]
    own = 2 * zl + c
    quad = [(zl if k < 2 else 1 - zl, c if k % 2 == 0 else 1 - c) for k in range(4)]
    root_y, root_zh = lax.div(x, 2), lax.rem(x, 2)
    dy = lax.rem(y + 4 - root_y, 4)
    in_root_zh = zh == root_zh
    home = [in_root_zh, jnp.logical_not(in_root_zh)]
    away = [home[1], home[0]]
    prim = jnp.where(in_root_zh, zl, 1 - zl)
    band = 2 * y + zh
    gives = y < 2
    shift = lax.rem(x + 8 - band, 4)
    units = [lax.rem(x + dy + j, 4) for j in range(4)]

    def at(y=y, zh=zh, zl=zl, x=x, c=c):
        return (y, zh, zl, x, c)

    relay = [at(y=lax.rem(y + shift, 4)), at(y=lax.rem(y + shift, 4), zh=1 - zh, zl=1 - zl)]
    source = at(x=units[0], y=root_y, zh=root_zh, zl=prim)
    at_home_0 = jnp.logical_and(in_root_zh, dy == 0)
    gives_away = [jnp.logical_and(gives, shift != 0), gives]
    diagonal = lax.rem(x + 4 - y, 4)
    is_relay, passes, passed_to, passed_from = [], [], [], []
    for g in range(2):
        zr = zh if g == 0 else 1 - zh
        second = jnp.where(diagonal == zr, 0, 1)
        target = zr + 2 * second
        on_path = jnp.logical_or(diagonal == zr, diagonal == zr + 1)
        moves = jnp.logical_and(on_path, x != target)
        is_relay.append(moves if g == 0 else on_path)
        passes.append(moves)
        passed_to.append(at(x=target))
        passed_from.append(at(y=second, zh=zr, zl=zl if g == 0 else 1 - zl))
    stays = jnp.logical_and(is_relay[1], jnp.logical_not(passes[1]))
    takes = [jnp.logical_and(in_root_zh, dy != 0), home[1]]
    arrives = [takes[0], jnp.logical_and(takes[1], dy != 0)]

    barrier = pltpu.get_barrier_semaphore()
    cross = at(zh=1 - zh, zl=1 - zl)
    opposite = at(zh=1 - zh)
    friends = [at(x=xs[d]) for d in range(1, 4)] + [at(y=ys[d]) for d in range(1, 4)] + [cross, opposite]
    friends += [at(zl=qz, c=qc) for qz, qc in quad[1:]]
    for f in friends:
        pl.semaphore_signal(barrier, inc=1, device_id=f, device_id_type=MESH)
    for g in range(2):
        guarded(gives_away[g], lambda: pl.semaphore_signal(barrier, inc=1, device_id=relay[g], device_id_type=MESH))
        guarded(is_relay[g], lambda: pl.semaphore_signal(barrier, inc=1, device_id=passed_from[g], device_id_type=MESH))
    count = sum(flag.astype(jnp.int32) for flag in gives_away + is_relay)
    for copy in fetch:
        copy.wait()

    def unpack(b, _):
        for q in range(72):
            o[pl.ds(b * 72 + q, 8, stride=PIECE), :] = planes[b, :, 128 * q:128 * q + 128]
        return 0

    lax.fori_loop(0, 6, unpack, 0)
    pl.semaphore_wait(barrier, len(friends) + count)

    m = Comm(ss, rs, fw.at[0, 0, 0])

    def orbital(ref, b):
        return ref.at[pl.ds(pl.multiple_of(b * PIECE, PIECE), PIECE)]


    def slots(*shape):
        return [slots(*shape[1:]) for _ in range(shape[0])] if shape else m.slot()

    S1, S2, S3 = slots(2, 4), slots(2, 2, 4), slots(2, 2, 2)
    JA, J1, ZP, ZS = (slots(2, CHUNKS) for _ in range(4))
    YR, DIE = (slots(2, CHUNKS, 2, 4) for _ in range(2))
    kind = [prim, 1 - prim]
    keep = [pltpu.make_async_copy(orbital(o, 2 * own + g), iv.at[g, piece(zl, x, c)], ls.at[g]) for g in range(2)]
    root_keep = pltpu.make_async_copy(orbital(o, 0), jv.at[0, piece(zl, x, c)], ls.at[2])

    def i_first(g):
        for k in range(1, 4):
            qz, qc = quad[k]
            m.send(orbital(o, 2 * (2 * qz + qc) + g), iv.at[g, piece(zl, x, c)], S1[g][k], at(zl=qz, c=qc))
        keep[g].start()

    def i_spread(g, k):
        rows = piece(quad[k][0], x, quad[k][1])
        src = iv.at[g, rows]
        if k == 0:
            src = orbital(o, 2 * own + g)
        else:
            m.wait(S1[g][k])
        for d in range(2):
            m.send(src, iv.at[g, rows], S2[g][d][k], at(x=xs[1 + 2 * d]))

    def i_forward(g):
        for kk in range(2):
            for d in range(2):
                k = kk + 2 * d
                rows = iv.at[g, piece(quad[k][0], xs[3 - 2 * d], quad[k][1])]
                m.wait(S2[g][d][k])
                m.send(rows, rows, S3[g][d][kk], at(x=xs[1 + 2 * d]))

    def i_finish(g):
        keep[g].wait()
        for d in range(2):
            for kk in range(2):
                m.wait(S2[g][d][kk + 2 - 2 * d])
                m.wait(S3[g][d][kk])

    stay = [pltpu.make_async_copy(hb.at[0, 1, h], jv.at[1, chunk(prim, units[0], c, h)], ls.at[6 + h]) for h in range(2)]

    def j_first(g):
        for h in range(CHUNKS):
            m.send(orbital(o, g).at[pl.ds(h * PART, PART)], hb.at[0, g, h], JA[g][h], relay[g], gives_away[g])
        if g == 0:
            guarded(at_home_0, root_keep.start)

    def j_relay(g, h):
        guarded(is_relay[g], lambda: m.wait(JA[g][h], PART))
        m.send(hb.at[0, g, h], jv.at[g, chunk(zl if g == 0 else 1 - zl, x, c, h)], J1[g][h], passed_to[g], passes[g])
        if g == 1:
            guarded(stays, stay[h].start)

    def j_row(g, kd, h):
        rows = jv.at[g, chunk(kind[kd], units[0], c, h)]
        for j in (1, 3):
            m.send(rows, rows, YR[g][h][kd][4 - j], at(y=ys[j]))
        m.send(rows, rows, DIE[g][h][kd][0], at(c=1 - c))

    def j_entry(g, h):
        rows = jv.at[g, chunk(prim, units[0], c, h)]
        if g == 0:
            if h == 0:
                guarded(at_home_0, root_keep.wait)
        else:
            guarded(stays, stay[h].wait)
        guarded(arrives[g], lambda: m.wait(J1[g][h], PART))
        m.send(rows, rows, ZP[g][h], cross, home[g])
        m.send(rows, rows, ZS[g][h], at(zl=1 - zl), home[g])
        m.send(rows, rows, ZS[g][h], opposite, home[g])
        guarded(away[g], lambda: m.wait(ZP[g][h], PART))
        j_row(g, 0, h)

    def j_other(g, h):
        m.wait(ZS[g][h], PART)
        j_row(g, 1, h)

    def j_take(g, h, kd, j, onward=None):
        rows = jv.at[g, chunk(kind[kd], units[j], c, h)]
        m.wait(YR[g][h][kd][j], PART)
        if onward:
            m.send(rows, rows, YR[g][h][kd][2], at(y=ys[onward]))
        m.send(rows, rows, DIE[g][h][kd][j], at(c=1 - c))

    def j_pass(g):
        for kd in range(2):
            j_take(g, 0, kd, 3, 1)
            j_take(g, 1, kd, 1, 3)

    def j_rows(g):
        for kd in range(2):
            j_take(g, 0, kd, 1)
            j_take(g, 1, kd, 3)
        for kd in range(2):
            for h in range(CHUNKS):
                j_take(g, h, kd, 2)

    def j_finish(g):
        for h in range(CHUNKS):
            for kd in range(2):
                for j in range(4):
                    m.wait(DIE[g][h][kd][j], PART)

    R1, R2, R4 = slots(2, 2, 2), slots(2, 2, 4), slots(2, 4)
    put = [pltpu.make_async_copy(nv.at[g, piece(zl, x, c)], orbital(out, 2 * own + g), ls.at[3 + g]) for g in range(2)]

    through = ((2, 0), (3, 1))

    def n_first(g):
        for kk in range(2):
            for d in range(2):
                k = through[d][kk]
                m.send(nv.at[g, piece(quad[k][0], xs[2], quad[k][1])], fw.at[g, d, kk], R1[g][d][kk], at(x=xs[1 + 2 * d]))
        for kk in range(2):
            for d in range(2):
                k = through[1 - d][kk]
                m.send(nv.at[g, piece(quad[k][0], xs[1 + 2 * d], quad[k][1])], rb.at[g, d, k], R2[g][d][k], at(x=xs[1 + 2 * d]))

    def n_second(g):
        for kk in range(2):
            for d in range(2):
                k = through[d][kk]
                m.wait(R1[g][d][kk])
                rows = nv.at[g, piece(quad[k][0], xs[1 + 2 * d], quad[k][1])]
                rows[...] += fw[g, d, kk]
                m.send(rows, rb.at[g, d, k], R2[g][d][k], at(x=xs[1 + 2 * d]))

    def n_third(g):
        for k in (2, 3, 1, 0):
            rows = nv.at[g, piece(quad[k][0], x, quad[k][1])]
            m.wait(R2[g][0][k])
            m.wait(R2[g][1][k])
            rows[...] += rb[g, 0, k] + rb[g, 1, k]
            if k == 0:
                put[g].start()
            else:
                m.send(rows, orbital(out, 2 * own + g), R4[g][k], at(zl=quad[k][0], c=quad[k][1]))

    def n_finish(g):
        for k in range(1, 4):
            m.wait(R4[g][k])
        put[g].wait()

    D1, D2, D3, D5, D6 = slots(2, 2, 4), slots(2, CHUNKS, 2, 4), slots(2, CHUNKS, 3), slots(2, CHUNKS), slots(2, CHUNKS)
    root_put = pltpu.make_async_copy(fv.at[0, piece(zl, x, c)], extra.at[0], ls.at[5])

    def f_first(g):
        for j in (2, 1, 3, 0):
            for kd in range(2):
                m.send(fv.at[g, piece(kind[kd], units[j], 1 - c)], db.at[g, kd, j], D1[g][kd][j], at(c=1 - c))

    def f_second(g, h):
        part = pl.ds(h * PART, PART)
        near_j = 1 if h == 0 else 3
        for j in (2, 4 - near_j, near_j, 0):
            for kd in (1, 0):
                rows = fv.at[g, chunk(kind[kd], units[j], c, h)]
                if h == 0:
                    m.wait(D1[g][kd][j])
                rows[...] += db[g, kd, j, part]
                if j == 2:
                    m.send(rows, yb.at[g, kd, 2, part], D2[g][h][kd][2], at(y=ys[near_j]))
                if j == 4 - near_j:
                    m.send(rows, yb.at[g, kd, j, part], D2[g][h][kd][j], at(y=ys[j]))

    def f_pass(g, h):
        part = pl.ds(h * PART, PART)
        near_j = 1 if h == 0 else 3
        for kd in (1, 0):
            rows = fv.at[g, chunk(kind[kd], units[near_j], c, h)]
            m.wait(D2[g][h][kd][2], PART)
            rows[...] += yb[g, kd, 2, part]
            m.send(rows, yb.at[g, kd, near_j, part], D2[g][h][kd][near_j], at(y=ys[near_j]))

    def f_third(g, h):
        part = pl.ds(h * PART, PART)
        for kd in (1, 0):
            rows = fv.at[g, chunk(kind[kd], units[0], c, h)]
            for j in (1, 3):
                m.wait(D2[g][h][kd][j], PART)
            rows[...] += yb[g, kd, 1, part] + yb[g, kd, 3, part]
            if kd:
                m.send(rows, zb.at[g, 0, part], D3[g][h][0], at(zl=1 - zl), home[g])
                m.send(rows, zb.at[g, 1, part], D3[g][h][1], opposite, away[g])
            else:
                m.send(rows, zb.at[g, 2, part], D3[g][h][2], cross, away[g])

    def f_fourth(g, h):
        part = pl.ds(h * PART, PART)
        rows = fv.at[g, chunk(prim, units[0], c, h)]

        def go():
            for e in range(3):
                m.wait(D3[g][h][e], PART)
            rows[...] += (zb[g, 0, part] + zb[g, 1, part]) + zb[g, 2, part]

        pl.when(home[g])(go)
        if g == 0 and h == CHUNKS - 1:
            guarded(at_home_0, root_put.start)
        m.send(rows, hb.at[1, g, h], D5[g][h], at(x=units[0]), arrives[g])
        if g == 1:
            m.send(rows, extra.at[g, part], D6[g][h], source, stays)

    def f_fifth(g, h):
        guarded(passes[g], lambda: m.wait(D5[g][h], PART))
        m.send(hb.at[1, g, h], extra.at[g, pl.ds(h * PART, PART)], D6[g][h], passed_from[g], passes[g])

    def f_finish(g):
        for h in range(CHUNKS):
            guarded(gives_away[g], lambda: m.wait(D6[g][h], PART))
        if g == 0:
            guarded(at_home_0, root_put.wait)

    j_first(0)
    i_first(0)
    i_spread(0, 0)
    j_first(1)
    i_first(1)
    build_kernel(k_ref)
    for k in range(1, 4):
        i_spread(0, k)
    j_relay(0, 0)
    j_relay(0, 1)
    j_entry(0, 0)
    j_relay(1, 0)
    j_entry(0, 1)
    j_relay(1, 1)
    i_spread(1, 0)
    j_other(0, 0)
    j_entry(1, 0)
    j_other(0, 1)
    j_entry(1, 1)
    i_forward(0)
    for k in range(1, 4):
        i_spread(1, k)
    j_pass(0)
    j_other(1, 0)
    j_other(1, 1)
    j_rows(0)
    i_finish(0)
    j_pass(1)
    j_finish(0)

    def do(*steps):
        def run():
            for step in steps:
                step()

        return run

    plan = {
        (0, 1): do(lambda: i_forward(1)),
        (0, 2): do(lambda: j_rows(1)),
        (1, 0): do(lambda: j_finish(1)),
        (2, 0): do(lambda: n_first(0), lambda: i_finish(1)),
        (3, 0): do(lambda: f_first(1), lambda: n_second(0)),
        (3, 2): do(lambda: f_second(1, 0), lambda: f_second(1, 1)),
    }

    def point(t, stage):
        for (tt, ss_), run in plan.items():
            if ss_ == stage:
                pl.when(t == tt)(run)

    transform_pairs(iv, jv, nv, fv, a, k_ref, wz_ref, wi_ref, ty_ref, tyi_ref, tx_ref, point)
    n_first(1)
    f_first(0)
    f_pass(1, 0)
    f_pass(1, 1)
    f_second(0, 0)
    f_second(0, 1)
    f_third(1, 0)
    f_third(1, 1)
    n_third(0)
    n_second(1)
    f_pass(0, 0)
    f_pass(0, 1)
    f_fourth(1, 0)
    f_fourth(1, 1)
    f_third(0, 0)
    f_third(0, 1)
    f_fifth(1, 0)
    f_fifth(1, 1)
    f_fourth(0, 0)
    f_fourth(0, 1)
    f_fifth(0, 0)
    f_fifth(0, 1)
    n_third(1)
    for g in range(2):
        n_finish(g)
        f_finish(g)

    for g in range(2):

        def add():
            out[pl.ds(g * PIECE, PIECE), :] += extra[g]

        pl.when(gives)(add)

    def pack(b, _):
        for q in range(72):
            planes[b, :, 128 * q:128 * q + 128] = out[pl.ds(b * 72 + q, 8, stride=PIECE), :]
        return 0

    lax.fori_loop(0, 6, pack, 0)
    stores = [pltpu.make_async_copy(planes.at[b], action.at[b], ls.at[8 + b]) for b in range(6)]
    for store in stores:
        store.start()
    m.finish()
    for store in stores:
        store.wait()


SENDS, RECEIVES = 256, 256


def local(orbitals):
    vm = pl.BlockSpec(memory_space=pltpu.VMEM)
    an = pl.BlockSpec(memory_space=pl.ANY)
    f32 = jnp.float32
    big = pltpu.VMEM((2, 6912, 128), f32)

    def pieces(*lead):
        return pltpu.VMEM(lead + (PIECE, 128), f32)

    return pl.pallas_call(
        exchange,
        out_shape=jax.ShapeDtypeStruct((6, 8, 9216), f32),
        in_specs=[an] + [vm] * 5,
        out_specs=an,
        scratch_shapes=[pltpu.VMEM((N * N, 128), f32), pltpu.VMEM((6, 8, 9216), f32), pltpu.VMEM((8 * PIECE, 128), f32), pltpu.VMEM((8 * PIECE, 128), f32), pieces(2), pltpu.VMEM((2, 2, CHUNKS, PART, 128), f32)]
        + [big] * 4
        + [pltpu.VMEM((96 * AS, 128), f32), pieces(2, 2, 2), pieces(2, 2, 4), pieces(2, 2, 4), pieces(2, 3), pieces(2, 2, 4)]
        + [pltpu.SemaphoreType.DMA((SENDS,)), pltpu.SemaphoreType.DMA((RECEIVES,)), pltpu.SemaphoreType.DMA((16,))],
        compiler_params=pltpu.CompilerParams(vmem_limit_bytes=67043328, collective_id=1, has_side_effects=True),
    )(orbitals.transpose(1, 0, 2), *tables()).transpose(1, 0, 2)


def solution(mesh):
    fine = jax.sharding.Mesh(mesh.devices.reshape(4, 2, 2, 4, 2), ("y", "zh", "zl", "x", "c"))
    placed = P(("y", "zh"), ("zl", "x", "c"), None)
    return jax.shard_map(local, mesh=fine, in_specs=(placed,), out_specs=placed, check_vma=False)
```
